32 devices in a mesh: seq: 4 (over z), fsdp: 8 (over y, x, core).
Axes of the slice: x: 2, y: 2, z: 4, core: 2. Of those that a mesh axis runs over, the one named last changes fastest.
Arguments:
- inputs: bfloat16 [8, 1024, 2048], P('fsdp', 'seq'), may hold values from -6 to 6
- norm1_gain: bfloat16 [2048], P(('seq', 'fsdp')), may hold values from 0.5 to 1.5
- w_query: bfloat16 [2048, 2048], P(('seq', 'fsdp')), may hold values from -0.125 to 0.125
- w_key: bfloat16 [2048, 2048], P(('seq', 'fsdp')), may hold values from -0.125 to 0.125
- w_value: bfloat16 [2048, 2048], P(('seq', 'fsdp')), may hold values from -0.125 to 0.125
- w_output: bfloat16 [2048, 2048], P(('seq', 'fsdp')), may hold values from -0.5 to 0.5
- norm2_gain: bfloat16 [2048], P(('seq', 'fsdp')), may hold values from 0.5 to 1.5
- w_gate: bfloat16 [2048, 8192], P(('seq', 'fsdp')), may hold values from -0.125 to 0.125
- w_up: bfloat16 [2048, 8192], P(('seq', 'fsdp')), may hold values from -0.125 to 0.125
- w_down: bfloat16 [8192, 2048], P(('seq', 'fsdp')), may hold values from -0.0625 to 0.0625
- out_grad: bfloat16 [8, 1024, 2048], P('fsdp', 'seq'), may hold values from -6 to 6
Outputs:
- output: bfloat16 [8, 1024, 2048], P('fsdp', 'seq')
- input_grad: float32 [8, 1024, 2048], P('fsdp', 'seq')
- norm1_gain_grad: float32 [2048], P(('seq', 'fsdp'))
- w_query_grad: float32 [2048, 2048], P(('seq', 'fsdp'))
- w_key_grad: float32 [2048, 2048], P(('seq', 'fsdp'))
- w_value_grad: float32 [2048, 2048], P(('seq', 'fsdp'))
- w_output_grad: float32 [2048, 2048], P(('seq', 'fsdp'))
- norm2_gain_grad: float32 [2048], P(('seq', 'fsdp'))
- w_gate_grad: float32 [2048, 8192], P(('seq', 'fsdp'))
- w_up_grad: float32 [2048, 8192], P(('seq', 'fsdp'))
- w_down_grad: float32 [8192, 2048], P(('seq', 'fsdp'))
The draws below stay inside these ranges and needn't reach their ends.
All inputs are finite; a program needn't handle non-finite values.
Results may differ from the reference program's by a relative error of at most 0.014.
Values may be sent and summed in bfloat16 or wider, within the bound.
No kernel may reach another device: no remote copies, remote signals or barrier semaphores. Data moves between devices by JAX's collectives and lax.ppermute only.
A program may use at most 576 MiB of HBM per device.

```python
import math
import jax
import jax.numpy as jnp
from jax import lax

D = 2048
HEADS = 32
HEAD_DIM = 64
FF = 8192
LEN = 1024
NSEQ_ALL = 8


def strengthened(drawn, stream_key, source, target, parts, factor):
    def block_of(axis_at):
        return (jnp.arange(drawn.shape[axis_at]) // (drawn.shape[axis_at] // parts)).reshape((-1,) + (1,) * (drawn.ndim - 1 - axis_at))

    first = jax.random.permutation(stream_key, parts)[block_of(target)]
    second = (block_of(target) + parts // 2) % parts
    return jnp.where((block_of(source) == first) | (block_of(source) == second), factor * drawn, drawn)


def levels(stream_key, dims, shards, low, high):
    level, own = 1.0, jax.random.fold_in(stream_key, 6)
    for dim, parts in shards:
        draws = jnp.exp(jax.random.uniform(jax.random.fold_in(own, dim), (parts,), jnp.float32, low / len(shards), high / len(shards)))
        level = level * jnp.repeat(draws, dims[dim] // parts).reshape([-1 if axis == dim else 1 for axis in range(len(dims))])
    return level


def bell_draw(rng, shape, width, limit, cuts=(), kind=jnp.bfloat16):
    entries = width * jax.random.normal(rng, shape, jnp.float32)
    if cuts:
        entries = entries * levels(rng, shape, cuts, -0.22, 0.18)
    return jnp.clip(entries, -limit, limit).astype(kind)


def gaussian_with(key, extent, deviation, most, shards, heavy, kind=jnp.bfloat16):
    values = deviation * jax.random.normal(key, extent, jnp.float32)
    if shards:
        values = values * levels(key, extent, shards, -0.22, 0.18)
    return jnp.clip(strengthened(values, jax.random.fold_in(key, 3), *heavy), -most, most).astype(kind)


def setup_inputs(seed: int = 0) -> dict:
    seeds = jax.random.split(jax.random.key(seed), 12)
    return {
        "inputs": gaussian_with(seeds[0], (NSEQ_ALL, LEN, D), 1.0, 6.0, ((0, 8), (1, 4)), (0, 2, 8, 2.0)),
        "norm1_gain": jnp.clip(1.0 + 0.1 * jax.random.normal(seeds[1], (D,), jnp.float32), 0.5, 1.5).astype(jnp.bfloat16),
        "w_query": bell_draw(seeds[2], (D, D), D ** -0.5, 0.125, ((0, 32),)),
        "w_key": bell_draw(seeds[3], (D, D), D ** -0.5, 0.125, ((0, 32),)),
        "w_value": bell_draw(seeds[4], (D, D), D ** -0.5, 0.125, ((0, 32),)),
        "w_output": bell_draw(seeds[5], (D, D), (D // 16) ** -0.5, 0.5, ((0, 32),)),
        "norm2_gain": jnp.clip(1.0 + 0.1 * jax.random.normal(seeds[6], (D,), jnp.float32), 0.5, 1.5).astype(jnp.bfloat16),
        "w_gate": bell_draw(seeds[7], (D, FF), D ** -0.5, 0.125, ((0, 32),)),
        "w_up": bell_draw(seeds[8], (D, FF), D ** -0.5, 0.125, ((0, 32),)),
        "w_down": bell_draw(seeds[9], (FF, D), FF ** -0.5, 0.0625, ((0, 32),)),
        "out_grad": gaussian_with(seeds[10], (NSEQ_ALL, LEN, D), 1.0, 6.0, ((0, 8), (1, 4)), (0, 2, 8, 2.0)),
    }


EPS = 1e-05
ROPE_BASE = 130000.0
NEG_FILL = -1e+30
HIGH = lax.Precision.HIGHEST

@jax.custom_vjp
def low(v):
    return lax.optimization_barrier(v.astype(jnp.bfloat16)).astype(jnp.float32)

@jax.custom_vjp
def low_back(v):
    return v

def low_keep(v):
    return (low(v), None)

def low_pass(kept, grad):
    return (grad,)

def back_keep(v):
    return (v, None)

def back_low(kept, grad):
    return (low(grad),)
low.defvjp(low_keep, low_pass)
low_back.defvjp(back_keep, back_low)

def tables(positions):
    half_dim = HEAD_DIM // 2
    freqs = jnp.exp(jnp.arange(half_dim, dtype=jnp.float32) * (-2.0 * math.log(ROPE_BASE) / HEAD_DIM))
    angle = positions.astype(jnp.float32)[:, None] * freqs[None, :]
    angle = jnp.concatenate([angle, angle], axis=1)
    return (jnp.cos(angle), jnp.sin(angle))

def rotate_half(values):
    half_dim = values.shape[-1] // 2
    return jnp.concatenate([-values[..., half_dim:], values[..., :half_dim]], axis=-1)

def matmul_hi(left, right):
    return jnp.dot(left, right, precision=HIGH)

def normalize(values, gain):
    inverse = lax.rsqrt(lax.optimization_barrier(jnp.mean(values * values, axis=-1, keepdims=True)) + EPS)
    return values * inverse * gain

def forward(inputs, gain_one, query_w, key_w, value_w, output_w, gain_two, gate_w, up_w, down_w):
    seq_len = inputs.shape[0]
    cosine, sine = tables(jnp.arange(seq_len, dtype=jnp.int32))

    def rotary(values):
        shaped = values.reshape(seq_len, HEADS, HEAD_DIM)
        return shaped * cosine[:, None, :] + rotate_half(shaped) * sine[:, None, :]
    normed_one = low(normalize(inputs, gain_one))
    queries = low_back(low(rotary(low_back(matmul_hi(normed_one, query_w)))))
    keys = low_back(low(rotary(low_back(matmul_hi(normed_one, key_w)))))
    values_h = low_back(low(matmul_hi(normed_one, value_w))).reshape(seq_len, HEADS, HEAD_DIM)
    scores = jnp.einsum('qhd,khd->hqk', queries, keys, precision=HIGH) * HEAD_DIM ** (-0.5)
    scores = low_back(scores)
    allowed = jnp.arange(seq_len)[None, :] <= jnp.arange(seq_len)[:, None]
    scores = jnp.where(allowed[None], scores, NEG_FILL)
    row_max = lax.optimization_barrier(jnp.max(scores, axis=-1, keepdims=True))
    shifted = jnp.exp(scores - row_max)
    attn_prob = low(shifted / lax.optimization_barrier(jnp.sum(shifted, axis=-1, keepdims=True)))
    attended = jnp.einsum('hqk,khd->qhd', attn_prob, values_h, precision=HIGH).reshape(seq_len, HEADS * HEAD_DIM)
    attended = low_back(low(attended))
    mid_stream = inputs + low_back(matmul_hi(attended, output_w))
    normed_two = low(normalize(mid_stream, gain_two))
    gate_pre = low_back(matmul_hi(normed_two, gate_w))
    up_pre = low_back(matmul_hi(normed_two, up_w))
    hidden = low(gate_pre * jax.nn.sigmoid(gate_pre) * up_pre)
    return mid_stream + low_back(matmul_hi(hidden, down_w))

def reference(inputs, norm1_gain, w_query, w_key, w_value, w_output, norm2_gain, w_gate, w_up, w_down, out_grad):
    params = tuple((param.astype(jnp.float32) for param in (norm1_gain, w_query, w_key, w_value, w_output, norm2_gain, w_gate, w_up, w_down)))

    def one_sequence(grad_sums, seq_pair):
        seq_in, seq_grad = seq_pair
        result, pullback = jax.vjp(forward, seq_in.astype(jnp.float32), *params)
        grad_list = pullback(seq_grad.astype(jnp.float32))
        grad_sums = tuple((total_part + new_part for total_part, new_part in zip(grad_sums, grad_list[1:])))
        return (grad_sums, (result.astype(jnp.bfloat16), grad_list[0]))
    zero_sums = tuple((jnp.zeros(param.shape, jnp.float32) for param in params))
    grad_sums, (output, input_grad) = lax.scan(one_sequence, zero_sums, (inputs, out_grad))
    return (output, input_grad, grad_sums[0], grad_sums[1], grad_sums[2], grad_sums[3], grad_sums[4], grad_sums[5], grad_sums[6], grad_sums[7], grad_sums[8])
```

```python
import functools
import math

import jax
import jax.numpy as jnp
from jax import lax
from jax.experimental import pallas as pl
from jax.experimental.pallas import tpu as pltpu
from jax.sharding import Mesh
from jax.sharding import PartitionSpec as P

HEAD_DIM = 64
HALF = HEAD_DIM // 2
SCALE = HEAD_DIM ** (-0.5)
EPS = 1e-05
ROPE_BASE = 130000.0
BF = jnp.bfloat16
F32 = jnp.float32


def dot(left, right, dims):
    return lax.dot_general(left, right, (dims, ((), ())), preferred_element_type=F32)


def mm(left, right):
    return dot(left, right, ((left.ndim - 1,), (0,)))


def mm_nt(left, right):
    return dot(left, right, ((left.ndim - 1,), (1,)))


def mm_tn(left, right):
    return dot(left, right, ((0,), (0,)))


def qk_head(width, head):
    lane = lax.broadcasted_iota(jnp.int32, (1, width), 1)
    return (lane % (width // 2)) // HALF == head


def v_head(width, head):
    return lax.broadcasted_iota(jnp.int32, (1, width), 1) // HEAD_DIM == head


def causal(rows):
    key = lax.broadcasted_iota(jnp.int32, (rows, rows), 0)
    query = lax.broadcasted_iota(jnp.int32, (rows, rows), 1)
    return key <= query


def attend_kernel(heads, ring, where_ref, qkv_ref, send_ref, keep_ref, lse_ref, key_ref, vt_ref, ot_ref):
    rows, width = qkv_ref.shape[1], qkv_ref.shape[2] // 3
    block = pl.program_id(1)
    z = where_ref[0]

    @pl.when(block == 0)
    def _():
        for p in range(ring):
            at = lax.rem(z - p + ring, ring)
            key_ref[p * rows : (p + 1) * rows] = qkv_ref[at, :, width : 2 * width]
            vt_ref[:, p * rows : (p + 1) * rows] = qkv_ref[at, :, 2 * width :].T

    def one(p):
        done = p * rows
        query = qkv_ref[lax.rem(z - p + ring, ring), :, :width]
        keep = causal(rows)
        for head in range(heads):
            query_h = jnp.where(qk_head(width, head), query, jnp.zeros_like(query))
            diag = dot(key_ref[done : done + rows], query_h, ((1,), (1,))) * SCALE
            diag = jnp.where(keep, diag, -1e30)
            top = jnp.max(diag, axis=0, keepdims=True)
            if p:
                past = dot(key_ref[:done], query_h, ((1,), (1,))) * SCALE
                top = jnp.maximum(top, jnp.max(past, axis=0, keepdims=True))
                past = jnp.exp(past - top)
            diag = jnp.exp(diag - top)
            total = jnp.sum(diag, axis=0, keepdims=True)
            if p:
                total = total + jnp.sum(past, axis=0, keepdims=True)
            share = 1.0 / total
            at = slice(head * HEAD_DIM, (head + 1) * HEAD_DIM)
            out = mm(vt_ref[at, done : done + rows], (diag * share).astype(BF))
            if p:
                out = out + mm(vt_ref[at, :done], (past * share).astype(BF))
            ot_ref[at] = out
            lse_ref[head : head + 1] = top + jnp.log(total)
        out = ot_ref[...].T.astype(BF)
        send_ref[...] = out
        keep_ref[...] = out

    for p in range(ring):
        pl.when(block == p)(functools.partial(one, p))


def attend(qkv, where, heads):
    ring, pair, rows, full = qkv.shape
    width = full // 3
    return pl.pallas_call(
        functools.partial(attend_kernel, heads, ring),
        out_shape=(
            jax.ShapeDtypeStruct((ring * pair, rows, width), BF),
            jax.ShapeDtypeStruct((ring, pair, rows, width), BF),
            jax.ShapeDtypeStruct((pair, ring, heads, rows), F32),
        ),
        grid_spec=pltpu.PrefetchScalarGridSpec(
            num_scalar_prefetch=1,
            grid=(pair, ring),
            in_specs=[pl.BlockSpec((ring, None, rows, full), lambda i, p, w: (0, i, 0, 0))],
            out_specs=[
                pl.BlockSpec((None, rows, width), lambda i, p, w: (p * pair + lax.rem(w[1] + i, pair), 0, 0)),
                pl.BlockSpec((None, None, rows, width), lambda i, p, w: (lax.rem(w[0] - p + ring, ring), i, 0, 0)),
                pl.BlockSpec((None, None, heads, rows), lambda i, p, w: (i, p, 0, 0)),
            ],
            scratch_shapes=[
                pltpu.VMEM((ring * rows, width), BF),
                pltpu.VMEM((width, ring * rows), BF),
                pltpu.VMEM((width, rows), F32),
            ],
        ),
        compiler_params=pltpu.CompilerParams(vmem_limit_bytes=48 << 20),
        cost_estimate=pl.CostEstimate(
            flops=2 * 2 * pair * heads * (ring * rows) ** 2 * width * 5 // 8,
            bytes_accessed=2 * qkv.size * 2,
            transcendentals=pair * heads * (ring * rows) ** 2,
        ),
        name="attend",
    )(where, qkv)


def attend_back_kernel(
    heads, ring, where_ref, qkv_ref, datt_ref, lse_ref, cos_ref, sin_ref, out_ref,
    key_ref, kt_ref, val_ref, qt_ref, dk_ref, dv_ref,
):
    rows, width = qkv_ref.shape[1], qkv_ref.shape[2] // 3
    half = width // 2
    block = pl.program_id(1)
    z = where_ref[0]

    @pl.when(block == 0)
    def _():
        for p in range(ring):
            at = lax.rem(z - p + ring, ring)
            key = qkv_ref[at, :, width : 2 * width]
            key_ref[p * rows : (p + 1) * rows] = key
            kt_ref[:, p * rows : (p + 1) * rows] = key.T
            val_ref[p * rows : (p + 1) * rows] = qkv_ref[at, :, 2 * width :]
        dk_ref[...] = jnp.zeros_like(dk_ref)
        dv_ref[...] = jnp.zeros_like(dv_ref)

    def turn_back(grad, p):
        cosine, sine = cos_ref[p * rows : (p + 1) * rows], sin_ref[p * rows : (p + 1) * rows]
        grad = grad.astype(BF).astype(F32)
        first, second = grad[:, :half], grad[:, half:]
        return (first * cosine + second * sine).astype(BF), (second * cosine - first * sine).astype(BF)

    def one(p):
        done = p * rows
        at = lax.rem(z - p + ring, ring)
        query = qkv_ref[at, :, :width]
        grad = datt_ref[...]
        keep = causal(rows)
        for head in range(heads):
            query_h = jnp.where(qk_head(width, head), query, jnp.zeros_like(query))
            grad_h = jnp.where(v_head(width, head), grad, jnp.zeros_like(grad))
            lse = lse_ref[head : head + 1]
            parts = []
            for low, high in ([(0, done)] if p else []) + [(done, done + rows)]:
                score = dot(key_ref[low:high], query_h, ((1,), (1,))) * SCALE
                prob = jnp.exp(score - lse)
                if low == done:
                    prob = jnp.where(keep, prob, 0.0)
                dprob = dot(val_ref[low:high], grad_h, ((1,), (1,)))
                parts.append((low, high, prob, dprob))
            delta = sum(jnp.sum(prob * dprob, axis=0, keepdims=True) for _, _, prob, dprob in parts)
            turned = 0.0
            for low, high, prob, dprob in parts:
                dscore = (prob * (dprob - delta)).astype(BF)
                key_t = jnp.concatenate(
                    [
                        kt_ref[head * HALF : (head + 1) * HALF, low:high],
                        kt_ref[half + head * HALF : half + (head + 1) * HALF, low:high],
                    ],
                    axis=0,
                )
                turned = turned + mm(key_t, dscore)
                dk_ref[low:high] += mm(dscore, query_h)
                dv_ref[low:high] += mm(prob.astype(BF), grad_h)
            qt_ref[head * HALF : (head + 1) * HALF] = turned[:HALF]
            qt_ref[half + head * HALF : half + (head + 1) * HALF] = turned[HALF:]
        first, second = turn_back(qt_ref[...].T * SCALE, p)
        out_ref[at, :, :half] = first
        out_ref[at, :, half:width] = second

    for p in range(ring):
        pl.when(block == p)(functools.partial(one, p))

    @pl.when(block == ring - 1)
    def _():
        for p in range(ring):
            at = lax.rem(z - p + ring, ring)
            first, second = turn_back(dk_ref[p * rows : (p + 1) * rows] * SCALE, p)
            out_ref[at, :, width : width + half] = first
            out_ref[at, :, width + half : 2 * width] = second
            out_ref[at, :, 2 * width :] = dv_ref[p * rows : (p + 1) * rows].astype(BF)


def attend_back(qkv, datt, lse, cosine, sine, where, heads):
    ring, pair, rows, full = qkv.shape
    width = full // 3
    return pl.pallas_call(
        functools.partial(attend_back_kernel, heads, ring),
        out_shape=jax.ShapeDtypeStruct(qkv.shape, BF),
        grid_spec=pltpu.PrefetchScalarGridSpec(
            num_scalar_prefetch=1,
            grid=(pair, ring),
            in_specs=[
                pl.BlockSpec((ring, None, rows, full), lambda i, p, w: (0, i, 0, 0)),
                pl.BlockSpec((None, rows, width), lambda i, p, w: (p * pair + lax.rem(w[1] + i, pair), 0, 0)),
                pl.BlockSpec((None, None, heads, rows), lambda i, p, w: (i, p, 0, 0)),
                pl.BlockSpec((ring * rows, width // 2), lambda i, p, w: (0, 0)),
                pl.BlockSpec((ring * rows, width // 2), lambda i, p, w: (0, 0)),
            ],
            out_specs=pl.BlockSpec((ring, None, rows, full), lambda i, p, w: (0, i, 0, 0)),
            scratch_shapes=[
                pltpu.VMEM((ring * rows, width), BF),
                pltpu.VMEM((width, ring * rows), BF),
                pltpu.VMEM((ring * rows, width), BF),
                pltpu.VMEM((width, rows), F32),
                pltpu.VMEM((ring * rows, width), F32),
                pltpu.VMEM((ring * rows, width), F32),
            ],
        ),
        compiler_params=pltpu.CompilerParams(vmem_limit_bytes=52 << 20),
        cost_estimate=pl.CostEstimate(
            flops=5 * 2 * pair * heads * (ring * rows) ** 2 * width * 5 // 8,
            bytes_accessed=4 * qkv.size * 2,
            transcendentals=pair * heads * (ring * rows) ** 2,
        ),
        name="attend_back",
    )(where, qkv, datt, lse, cosine, sine)


def unit(values):
    inverse = lax.rsqrt(jnp.mean(values * values, axis=1, keepdims=True) + EPS)
    return values * inverse, inverse


def unit_back(grad, normed, inverse):
    return inverse * (grad - normed * jnp.mean(grad * normed, axis=1, keepdims=True))


def local(ring, plane, pair, inputs, norm1_gain, w_query, w_key, w_value, w_output, norm2_gain, w_gate, w_up, w_down, out_grad):
    seq_count, rows, model = inputs.shape
    parts = ring * pair
    own = w_query.shape[0]
    ff_own = w_down.shape[0]
    width = model // parts
    heads = width // HEAD_DIM
    half = width // 2
    ff = plane * ff_own
    group = ("seq", "core")
    z = lax.axis_index("seq")
    where = jnp.stack([z, lax.axis_index("core")]).astype(jnp.int32)
    ring_pairs = [(i, (i + 1) % ring) for i in range(ring)]
    core_pairs = [(i, (i + 1) % pair) for i in range(pair)]

    def hop(x):
        return lax.ppermute(x, "seq", ring_pairs)

    def swap(x):
        return lax.ppermute(x, "core", core_pairs)

    def ring_gather(x):
        blocks = [x]
        for _ in range(ring - 1):
            blocks.append(hop(blocks[-1]))
        return [jnp.stack([b, swap(b)]) for b in blocks]

    def ring_sum(terms):
        shares = [t[0].astype(F32) + swap(t[1]).astype(F32) for t in terms]
        total = shares[1].astype(BF)
        for k in range(2, ring):
            total = (hop(total).astype(F32) + shares[k]).astype(BF)
        return hop(total).astype(F32) + shares[0]

    def exchange(x):
        return lax.all_to_all(x, group, 0, 0, tiled=True)

    def plane_gather(x):
        return lax.all_gather(x, "yx", axis=0, tiled=True)

    def plane_sum(x):
        return lax.psum_scatter(x.astype(BF), "yx", scatter_dimension=0, tiled=True)

    def to_rows(x):
        return x.reshape(rows, ring, plane, pair * own).transpose(0, 2, 1, 3).reshape(rows, model)

    def from_rows(x):
        return x.reshape(rows, plane, ring, pair * own).transpose(0, 2, 1, 3).reshape(rows, model)

    def halves_out(w):
        return w.reshape(own, parts, heads, 2, HALF).transpose(1, 0, 3, 2, 4).reshape(parts, own, width)

    def halves_back(w):
        return w.reshape(parts, own, 2, heads, HALF).transpose(1, 0, 3, 2, 4).reshape(own, model)

    def heads_out(w):
        return w.reshape(own, parts, width).transpose(1, 0, 2)

    def heads_back(w):
        return w.transpose(1, 0, 2).reshape(own, model)

    def ff_out(w):
        return w.reshape(own, ring, plane, pair, ff_own).transpose(1, 3, 0, 2, 4).reshape(parts, own, ff)

    def ff_back(w):
        return w.reshape(ring, pair, own, plane, ff_own).transpose(2, 0, 3, 1, 4).reshape(own, parts * ff)

    gain_one, gain_two = norm1_gain.astype(F32)[:, None], norm2_gain.astype(F32)[:, None]

    def scaled(w, gain):
        return (w.astype(F32) * gain).astype(BF)

    qkv_w = exchange(
        jnp.concatenate(
            [halves_out(scaled(w_query, gain_one)), halves_out(scaled(w_key, gain_one)), heads_out(scaled(w_value, gain_one))],
            axis=2,
        )
    )
    qkv_w = plane_gather(qkv_w.reshape(parts * own, 3 * width))
    down_w = plane_gather(w_down)
    output_w = lax.all_gather(w_output, ("seq", "yx", "core"), axis=0, tiled=True)
    ff_w = exchange(jnp.concatenate([ff_out(scaled(w_gate, gain_two)), ff_out(scaled(w_up, gain_two))], axis=2))
    ff_w = plane_gather(ff_w.reshape(parts * own, 2 * ff))

    residual = inputs.reshape(rows, model).astype(F32)
    normed_one, inverse_one = unit(residual)
    ones = ring_gather(to_rows(normed_one.astype(BF)))

    freqs = jnp.exp(jnp.arange(HALF, dtype=F32) * (-2.0 * math.log(ROPE_BASE) / HEAD_DIM))
    angle = jnp.arange(ring * rows, dtype=jnp.int32).astype(F32)[:, None] * freqs[None, :]
    cosine, sine = jnp.tile(jnp.cos(angle), (1, heads)), jnp.tile(jnp.sin(angle), (1, heads))
    qkv = []
    for k in range(ring):
        start = lax.rem(z - k + ring, ring) * rows
        cos_k = lax.dynamic_slice_in_dim(cosine, start, rows)
        sin_k = lax.dynamic_slice_in_dim(sine, start, rows)
        flat = mm(ones[k].reshape(pair * rows, model), qkv_w).reshape(pair, rows, 3 * width)
        q1, q2 = flat[..., :half], flat[..., half:width]
        k1, k2 = flat[..., width : width + half], flat[..., width + half : 2 * width]
        qkv.append(
            jnp.concatenate(
                [
                    q1 * cos_k - q2 * sin_k,
                    q2 * cos_k + q1 * sin_k,
                    k1 * cos_k - k2 * sin_k,
                    k2 * cos_k + k1 * sin_k,
                    flat[..., 2 * width :],
                ],
                axis=-1,
            ).astype(BF)
        )
    qkv = jnp.stack(qkv)
    att_send, att_keep, lse = attend(qkv, where, heads)
    att = exchange(att_send).transpose(1, 0, 2).reshape(rows, model)
    mid = residual + mm(att, output_w)

    normed_two, inverse_two = unit(mid)
    twos = ring_gather(to_rows(normed_two.astype(BF)))
    grad_out = out_grad.reshape(rows, model)
    douts = ring_gather(grad_out)
    out_terms, two_terms, hiddens, dffs = [], [], [], []
    for k in range(ring):
        two, dout = twos[k].reshape(pair * rows, model), douts[k].reshape(pair * rows, model)
        both = mm(two, ff_w)
        gate, up = both[:, :ff], both[:, ff:]
        sig = jax.nn.sigmoid(gate)
        hidden = (gate * sig * up).astype(BF)
        out_terms.append(mm(hidden, down_w).astype(BF).reshape(pair, rows, model))
        dhid = mm_nt(dout, down_w)
        dgate = (dhid * up * sig * (1.0 + gate * (1.0 - sig))).astype(BF)
        dup = (dhid * gate * sig).astype(BF)
        dff = jnp.concatenate([dgate, dup], axis=1)
        two_terms.append(mm_nt(dff, ff_w).astype(BF).reshape(pair, rows, model))
        hiddens.append(hidden)
        dffs.append(dff)
    grad_two = from_rows(ring_sum(two_terms))
    output = (mid + ring_sum(out_terms)).astype(BF).reshape(inputs.shape)
    tokens = ring * pair * rows
    twos, douts = jnp.stack(twos).reshape(tokens, model), jnp.stack(douts).reshape(tokens, model)
    down_grad = plane_sum(mm_tn(jnp.concatenate(hiddens), douts)).astype(F32)
    ff_grad = plane_sum(mm_tn(twos, jnp.concatenate(dffs)))
    ff_grad = exchange(ff_grad.reshape(parts, own, 2 * ff)).astype(F32)
    gate_hat, up_hat = ff_back(ff_grad[..., :ff]), ff_back(ff_grad[..., ff:])
    gain_two_grad = jnp.sum(w_gate.astype(F32) * gate_hat + w_up.astype(F32) * up_hat, axis=1)

    grad_mid = grad_out.astype(F32) + unit_back(grad_two, normed_two, inverse_two)
    proj = grad_mid.astype(BF)
    datt = mm_nt(proj, output_w).astype(BF)
    datt = exchange(datt.reshape(rows, parts, width).transpose(1, 0, 2))
    dqkv = attend_back(qkv, datt, lse, cosine, sine, where, heads)
    projs = jnp.stack(ring_gather(proj)).reshape(tokens, model)
    output_grad = plane_sum(mm_tn(att_keep.reshape(tokens, width), projs)).astype(BF)
    moves = [(y * pair + c, c * plane + y) for y in range(plane) for c in range(pair)]
    output_grad = lax.ppermute(output_grad, ("yx", "core"), moves).astype(F32)

    one_terms = [mm_nt(dqkv[k].reshape(pair * rows, 3 * width), qkv_w).astype(BF).reshape(pair, rows, model) for k in range(ring)]
    ones = jnp.stack(ones).reshape(tokens, model)
    qkv_grad = plane_sum(mm_tn(ones, dqkv.reshape(tokens, 3 * width)))
    qkv_grad = exchange(qkv_grad.reshape(parts, own, 3 * width)).astype(F32)
    query_hat = halves_back(qkv_grad[..., :width])
    key_hat = halves_back(qkv_grad[..., width : 2 * width])
    value_hat = heads_back(qkv_grad[..., 2 * width :])
    gain_one_grad = jnp.sum(
        w_query.astype(F32) * query_hat + w_key.astype(F32) * key_hat + w_value.astype(F32) * value_hat, axis=1
    )
    grad_one = from_rows(ring_sum(one_terms))
    input_grad = (grad_mid + unit_back(grad_one, normed_one, inverse_one)).reshape(inputs.shape)
    return (
        output,
        input_grad,
        gain_one_grad,
        query_hat * gain_one,
        key_hat * gain_one,
        value_hat * gain_one,
        output_grad,
        gain_two_grad,
        gate_hat * gain_two,
        up_hat * gain_two,
        down_grad,
    )


def solution(mesh):
    ring, fsdp = mesh.shape["seq"], mesh.shape["fsdp"]
    pair = 2
    plane = fsdp // pair
    fine = Mesh(mesh.devices.reshape(ring, plane, pair), ("seq", "yx", "core"))
    tokens = P(("yx", "core"), "seq", None)
    every = ("seq", "yx", "core")
    weight, gain = P(every, None), P(every)
    return jax.shard_map(
        functools.partial(local, ring, plane, pair),
        mesh=fine,
        in_specs=(tokens, gain, weight, weight, weight, weight, gain, weight, weight, weight, tokens),
        out_specs=(tokens, tokens, gain, weight, weight, weight, weight, gain, weight, weight, weight),
        check_vma=False,
    )
```

```python
import functools
import math

import jax
import jax.numpy as jnp
from jax import lax
from jax.experimental import pallas as pl
from jax.experimental.pallas import tpu as pltpu
from jax.sharding import Mesh
from jax.sharding import PartitionSpec as P

HEAD_DIM = 64
HALF = HEAD_DIM // 2
SCALE = HEAD_DIM ** (-0.5)
EPS = 1e-05
ROPE_BASE = 130000.0
BF = jnp.bfloat16
F32 = jnp.float32
QUICK = pl.CostEstimate(flops=1, bytes_accessed=1, transcendentals=0)


def dot(left, right, dims):
    return lax.dot_general(left, right, (dims, ((), ())), preferred_element_type=F32)


def mm(left, right):
    return dot(left, right, ((left.ndim - 1,), (0,)))


def mm_nt(left, right):
    return dot(left, right, ((left.ndim - 1,), (1,)))


def mm_tn(left, right):
    return dot(left, right, ((0,), (0,)))


def qk_head(width, head):
    lane = lax.broadcasted_iota(jnp.int32, (1, width), 1)
    return (lane % (width // 2)) // HALF == head


def v_head(width, head):
    return lax.broadcasted_iota(jnp.int32, (1, width), 1) // HEAD_DIM == head


def causal(rows):
    key = lax.broadcasted_iota(jnp.int32, (rows, rows), 0)
    query = lax.broadcasted_iota(jnp.int32, (rows, rows), 1)
    return key <= query


def attend_kernel(heads, ring, where_ref, qkv_ref, send_ref, lse_ref, key_ref, vt_ref, ot_ref):
    rows, width = qkv_ref.shape[1], qkv_ref.shape[2] // 3
    block = pl.program_id(1)
    z = where_ref[0]

    @pl.when(block == 0)
    def _():
        for p in range(ring):
            at = lax.rem(z - p + ring, ring)
            key_ref[p * rows : (p + 1) * rows] = qkv_ref[at, :, width : 2 * width]
            vt_ref[:, p * rows : (p + 1) * rows] = qkv_ref[at, :, 2 * width :].T

    def one(p):
        done = p * rows
        query = qkv_ref[lax.rem(z - p + ring, ring), :, :width]
        keep = causal(rows)
        for head in range(heads):
            query_h = jnp.where(qk_head(width, head), query, jnp.zeros_like(query))
            diag = dot(key_ref[done : done + rows], query_h, ((1,), (1,))) * SCALE
            diag = jnp.where(keep, diag, -1e30)
            top = jnp.max(diag, axis=0, keepdims=True)
            if p:
                past = dot(key_ref[:done], query_h, ((1,), (1,))) * SCALE
                top = jnp.maximum(top, jnp.max(past, axis=0, keepdims=True))
                past = jnp.exp(past - top)
            diag = jnp.exp(diag - top)
            total = jnp.sum(diag, axis=0, keepdims=True)
            if p:
                total = total + jnp.sum(past, axis=0, keepdims=True)
            share = 1.0 / total
            at = slice(head * HEAD_DIM, (head + 1) * HEAD_DIM)
            out = mm(vt_ref[at, done : done + rows], (diag * share).astype(BF))
            if p:
                out = out + mm(vt_ref[at, :done], (past * share).astype(BF))
            ot_ref[at] = out
            lse_ref[head : head + 1] = top + jnp.log(total)
        send_ref[...] = ot_ref[...].T.astype(BF)

    for p in range(ring):
        pl.when(block == p)(functools.partial(one, p))


def attend(qkv, where, heads):
    ring, pair, rows, full = qkv.shape
    width = full // 3
    return pl.pallas_call(
        functools.partial(attend_kernel, heads, ring),
        out_shape=(
            jax.ShapeDtypeStruct((ring * pair, rows, width), BF),
            jax.ShapeDtypeStruct((pair, ring, heads, rows), F32),
        ),
        grid_spec=pltpu.PrefetchScalarGridSpec(
            num_scalar_prefetch=1,
            grid=(pair, ring),
            in_specs=[pl.BlockSpec((ring, None, rows, full), lambda i, p, w: (0, i, 0, 0))],
            out_specs=[
                pl.BlockSpec((None, rows, width), lambda i, p, w: (p * pair + lax.rem(w[1] + i, pair), 0, 0)),
                pl.BlockSpec((None, None, heads, rows), lambda i, p, w: (i, p, 0, 0)),
            ],
            scratch_shapes=[
                pltpu.VMEM((ring * rows, width), BF),
                pltpu.VMEM((width, ring * rows), BF),
                pltpu.VMEM((width, rows), F32),
            ],
        ),
        compiler_params=pltpu.CompilerParams(vmem_limit_bytes=48 << 20),
        cost_estimate=pl.CostEstimate(flops=20 * 10**9, bytes_accessed=2 * qkv.size * 2, transcendentals=0),
        name="attend",
    )(where, qkv)


def attend_back_kernel(
    heads, ring, where_ref, qkv_ref, datt_ref, lse_ref, cos_ref, sin_ref, out_ref,
    key_ref, kt_ref, val_ref, qt_ref, dk_ref, dv_ref,
):
    rows, width = qkv_ref.shape[1], qkv_ref.shape[2] // 3
    half = width // 2
    block = pl.program_id(1)
    z = where_ref[0]

    @pl.when(block == 0)
    def _():
        for p in range(ring):
            at = lax.rem(z - p + ring, ring)
            key = qkv_ref[at, :, width : 2 * width]
            key_ref[p * rows : (p + 1) * rows] = key
            kt_ref[:, p * rows : (p + 1) * rows] = key.T
            val_ref[p * rows : (p + 1) * rows] = qkv_ref[at, :, 2 * width :]
        dk_ref[...] = jnp.zeros_like(dk_ref)
        dv_ref[...] = jnp.zeros_like(dv_ref)

    def turn_back(grad, p):
        cosine, sine = cos_ref[p * rows : (p + 1) * rows], sin_ref[p * rows : (p + 1) * rows]
        grad = grad.astype(BF).astype(F32)
        first, second = grad[:, :half], grad[:, half:]
        return (first * cosine + second * sine).astype(BF), (second * cosine - first * sine).astype(BF)

    def one(p):
        done = p * rows
        at = lax.rem(z - p + ring, ring)
        query = qkv_ref[at, :, :width]
        grad = datt_ref[...]
        keep = causal(rows)
        for head in range(heads):
            query_h = jnp.where(qk_head(width, head), query, jnp.zeros_like(query))
            grad_h = jnp.where(v_head(width, head), grad, jnp.zeros_like(grad))
            lse = lse_ref[head : head + 1]
            parts = []
            for low, high in ([(0, done)] if p else []) + [(done, done + rows)]:
                score = dot(key_ref[low:high], query_h, ((1,), (1,))) * SCALE
                prob = jnp.exp(score - lse)
                if low == done:
                    prob = jnp.where(keep, prob, 0.0)
                dprob = dot(val_ref[low:high], grad_h, ((1,), (1,)))
                parts.append((low, high, prob, dprob))
            delta = sum(jnp.sum(prob * dprob, axis=0, keepdims=True) for _, _, prob, dprob in parts)
            turned = 0.0
            for low, high, prob, dprob in parts:
                dscore = (prob * (dprob - delta)).astype(BF)
                key_t = jnp.concatenate(
                    [
                        kt_ref[head * HALF : (head + 1) * HALF, low:high],
                        kt_ref[half + head * HALF : half + (head + 1) * HALF, low:high],
                    ],
                    axis=0,
                )
                turned = turned + mm(key_t, dscore)
                dk_ref[low:high] += mm(dscore, query_h)
                dv_ref[low:high] += mm(prob.astype(BF), grad_h)
            qt_ref[head * HALF : (head + 1) * HALF] = turned[:HALF]
            qt_ref[half + head * HALF : half + (head + 1) * HALF] = turned[HALF:]
        first, second = turn_back(qt_ref[...].T * SCALE, p)
        out_ref[at, :, :half] = first
        out_ref[at, :, half:width] = second

    for p in range(ring):
        pl.when(block == p)(functools.partial(one, p))

    @pl.when(block == ring - 1)
    def _():
        for p in range(ring):
            at = lax.rem(z - p + ring, ring)
            first, second = turn_back(dk_ref[p * rows : (p + 1) * rows] * SCALE, p)
            out_ref[at, :, width : width + half] = first
            out_ref[at, :, width + half : 2 * width] = second
            out_ref[at, :, 2 * width :] = dv_ref[p * rows : (p + 1) * rows].astype(BF)


def attend_back(qkv, datt, lse, cosine, sine, where, heads):
    ring, pair, rows, full = qkv.shape
    width = full // 3
    return pl.pallas_call(
        functools.partial(attend_back_kernel, heads, ring),
        out_shape=jax.ShapeDtypeStruct(qkv.shape, BF),
        grid_spec=pltpu.PrefetchScalarGridSpec(
            num_scalar_prefetch=1,
            grid=(pair, ring),
            in_specs=[
                pl.BlockSpec((ring, None, rows, full), lambda i, p, w: (0, i, 0, 0)),
                pl.BlockSpec((None, rows, width), lambda i, p, w: (p * pair + lax.rem(w[1] + i, pair), 0, 0)),
                pl.BlockSpec((None, None, heads, rows), lambda i, p, w: (i, p, 0, 0)),
                pl.BlockSpec((ring * rows, width // 2), lambda i, p, w: (0, 0)),
                pl.BlockSpec((ring * rows, width // 2), lambda i, p, w: (0, 0)),
            ],
            out_specs=pl.BlockSpec((ring, None, rows, full), lambda i, p, w: (0, i, 0, 0)),
            scratch_shapes=[
                pltpu.VMEM((ring * rows, width), BF),
                pltpu.VMEM((width, ring * rows), BF),
                pltpu.VMEM((ring * rows, width), BF),
                pltpu.VMEM((width, rows), F32),
                pltpu.VMEM((ring * rows, width), F32),
                pltpu.VMEM((ring * rows, width), F32),
            ],
        ),
        compiler_params=pltpu.CompilerParams(vmem_limit_bytes=52 << 20),
        cost_estimate=pl.CostEstimate(flops=28 * 10**9, bytes_accessed=4 * qkv.size * 2, transcendentals=0),
        name="attend_back",
    )(where, qkv, datt, lse, cosine, sine)


def feed_kernel(
    steps, two_ref, two_other_ref, dout_ref, dout_other_ref, ff_in_ref, down_in_ref, ff_back_ref, down_out_ref, *refs,
):
    x_ref, dy_ref, hidden_ref, dff_ref, out_ref, out_other_ref, back_ref, back_other_ref = refs[-8:]
    rows = two_ref.shape[0]
    chunk = down_in_ref.shape[0]
    step = pl.program_id(0)

    @pl.when(step == 0)
    def _():
        x_ref[:rows], x_ref[rows:] = two_ref[...], two_other_ref[...]
        dy_ref[:rows], dy_ref[rows:] = dout_ref[...], dout_other_ref[...]

    def hidden_units(j):
        both = mm(x_ref[...], ff_in_ref[...])
        dhid = mm_nt(dy_ref[...], down_in_ref[...])
        gate, up = both[:, :chunk], both[:, chunk:]
        sig = jax.nn.sigmoid(gate)
        act = gate * sig
        hidden_ref[:, j * chunk : (j + 1) * chunk] = (act * up).astype(BF)
        dgate = dhid * up * (sig * (1.0 + gate * (1.0 - sig)))
        dff_ref[:, 2 * j * chunk : (2 * j + 1) * chunk] = dgate.astype(BF)
        dff_ref[:, (2 * j + 1) * chunk : (2 * j + 2) * chunk] = (dhid * act).astype(BF)

    for j in range(steps):
        pl.when(step == j)(functools.partial(hidden_units, j))

    @pl.when(step >= steps)
    def _():
        out = mm(hidden_ref[...], down_out_ref[...]).astype(BF)
        out_ref[...], out_other_ref[...] = out[:rows], out[rows:]
        back = mm_nt(dff_ref[...], ff_back_ref[...]).astype(BF)
        back_ref[...], back_other_ref[...] = back[:rows], back[rows:]


def feed(k, blocks, kept, two, two_other, dout, dout_other, ff_w, down_w, chunk):
    rows, model = two.shape
    ff = down_w.shape[0]
    steps = ff // chunk
    part = model // steps
    whole = pl.BlockSpec((rows, model), lambda j: (0, 0))
    share = pl.BlockSpec((rows, part), lambda j: (0, jnp.maximum(j - steps, 0)))
    widths = (model, model, ff, 2 * ff)
    *kept, out, out_other, back, back_other = pl.pallas_call(
        functools.partial(feed_kernel, steps),
        out_shape=[jax.ShapeDtypeStruct((blocks * 2 * rows, w), BF) for w in widths] + [jax.ShapeDtypeStruct((rows, model), BF)] * 4,
        grid=(2 * steps,),
        in_specs=[
            whole, whole, whole, whole,
            pl.BlockSpec((model, 2 * chunk), lambda j: (0, jnp.minimum(j, steps - 1))),
            pl.BlockSpec((chunk, model), lambda j: (jnp.minimum(j, steps - 1), 0)),
            pl.BlockSpec((part, 2 * ff), lambda j: (jnp.maximum(j - steps, 0), 0)),
            pl.BlockSpec((ff, part), lambda j: (0, jnp.maximum(j - steps, 0))),
        ] + [pl.BlockSpec(memory_space=pl.ANY)] * len(kept),
        out_specs=[pl.BlockSpec((2 * rows, w), lambda j: (k, 0)) for w in widths] + [share] * 4,
        input_output_aliases={8 + i: i for i in range(len(kept))},
        compiler_params=pltpu.CompilerParams(vmem_limit_bytes=56 << 20),
        cost_estimate=pl.CostEstimate(flops=2 * rows * model * ff * 6, bytes_accessed=1, transcendentals=0),
        name="feed",
    )(two, two_other, dout, dout_other, ff_w, down_w, ff_w, down_w, *kept)
    return kept, (out, out_other), (back, back_other)


def project_kernel(where_ref, one_ref, other_ref, w_ref, cos_ref, sin_ref, *refs):
    x_ref, out_ref = refs[-2:]
    rows = one_ref.shape[0]
    half = w_ref.shape[1] // 2
    step = pl.program_id(0)

    @pl.when(step == 0)
    def _():
        x_ref[:rows], x_ref[rows:] = one_ref[...], other_ref[...]

    flat = mm(x_ref[...], w_ref[...])

    @pl.when(step < 2)
    def _():
        cosine, sine = cos_ref[...], sin_ref[...]
        for i in range(2):
            first, second = flat[i * rows : (i + 1) * rows, :half], flat[i * rows : (i + 1) * rows, half:]
            out_ref[i, :, :half] = (first * cosine - second * sine).astype(BF)
            out_ref[i, :, half:] = (second * cosine + first * sine).astype(BF)

    @pl.when(step == 2)
    def _():
        out_ref[0], out_ref[1] = flat[:rows].astype(BF), flat[rows:].astype(BF)


def project(k, blocks, kept, where, one, other, w, cosine, sine):
    rows, model = one.shape
    width = w.shape[1] // 3
    whole = pl.BlockSpec((rows, model), lambda j, at: (0, 0))
    table = pl.BlockSpec((rows, width // 2), lambda j, at: (lax.rem(at[0] - k + blocks, blocks), 0))
    return pl.pallas_call(
        project_kernel,
        out_shape=(
            jax.ShapeDtypeStruct((blocks * 2 * rows, model), BF),
            jax.ShapeDtypeStruct((blocks, 2, rows, 3 * width), BF),
        ),
        grid_spec=pltpu.PrefetchScalarGridSpec(
            num_scalar_prefetch=1,
            grid=(3,),
            in_specs=[whole, whole, pl.BlockSpec((model, width), lambda j, at: (0, j)), table, table]
            + [pl.BlockSpec(memory_space=pl.ANY)] * len(kept),
            out_specs=(
                pl.BlockSpec((2 * rows, model), lambda j, at: (k, 0)),
                pl.BlockSpec((None, 2, rows, width), lambda j, at: (k, 0, 0, j)),
            ),
        ),
        input_output_aliases={6 + i: i for i in range(len(kept))},
        compiler_params=pltpu.CompilerParams(vmem_limit_bytes=40 << 20),
        cost_estimate=QUICK,
        name="project",
    )(where, one, other, w, cosine, sine, *kept)


def ff_out_kernel(turn, gain_ref, gate_ref, up_ref, out_ref):
    pair = out_ref.shape[0]
    gain = gain_ref[...]
    for y in range(out_ref.shape[2] // (2 * turn)):
        for c in range(pair):
            at = (y * pair + c) * turn
            for i, ref in enumerate((gate_ref, up_ref)):
                cols = (ref[:, at : at + turn].astype(F32) * gain).astype(BF)
                out_ref[c, :, (2 * y + i) * turn : (2 * y + i + 1) * turn] = cols


def ff_out(ring, pair, turn, gain, w_gate, w_up):
    own, full = w_gate.shape
    part = pl.BlockSpec((own, full // ring), lambda s: (0, s))
    return pl.pallas_call(
        functools.partial(ff_out_kernel, turn),
        out_shape=jax.ShapeDtypeStruct((ring * pair, own, 2 * full // (ring * pair)), BF),
        grid=(ring,),
        in_specs=[pl.BlockSpec((own, 1), lambda s: (0, 0)), part, part],
        out_specs=pl.BlockSpec((pair, own, 2 * full // (ring * pair)), lambda s: (s, 0, 0)),
        cost_estimate=pl.CostEstimate(flops=1, bytes_accessed=8 * w_gate.size, transcendentals=0),
        name="ff_out",
    )(gain, w_gate, w_up)


def ff_back_kernel(turn, gain_ref, hat_ref, gate_ref, up_ref, gate_out, up_out, sum_ref):
    pair = hat_ref.shape[0]
    gain = gain_ref[...]
    total = jnp.zeros(gain.shape, F32)
    for y in range(hat_ref.shape[2] // (2 * turn)):
        for c in range(pair):
            at = (y * pair + c) * turn
            for i, (ref, out) in enumerate(((gate_ref, gate_out), (up_ref, up_out))):
                hat = hat_ref[c, :, (2 * y + i) * turn : (2 * y + i + 1) * turn].astype(F32)
                total += jnp.sum(hat * ref[:, at : at + turn].astype(F32), axis=1, keepdims=True)
                out[:, at : at + turn] = hat * gain

    @pl.when(pl.program_id(0) == 0)
    def _():
        sum_ref[...] = total

    @pl.when(pl.program_id(0) > 0)
    def _():
        sum_ref[...] += total


def ff_back(ring, turn, gain, hat, w_gate, w_up):
    own, full = w_gate.shape
    pair = hat.shape[0] // ring
    part = pl.BlockSpec((own, full // ring), lambda s: (0, s))
    column = pl.BlockSpec((own, 1), lambda s: (0, 0))
    return pl.pallas_call(
        functools.partial(ff_back_kernel, turn),
        out_shape=(jax.ShapeDtypeStruct((own, full), F32),) * 2 + (jax.ShapeDtypeStruct((own, 1), F32),),
        grid=(ring,),
        in_specs=[column, pl.BlockSpec((pair, *hat.shape[1:]), lambda s: (s, 0, 0)), part, part],
        out_specs=(part, part, column),
        cost_estimate=pl.CostEstimate(flops=1, bytes_accessed=16 * w_gate.size, transcendentals=0),
        name="ff_back",
    )(gain, hat, w_gate, w_up)


def qkv_out_kernel(gain_ref, query_ref, key_ref, value_ref, out_ref):
    width = query_ref.shape[1]
    gain = gain_ref[...]
    for i, ref in enumerate((query_ref, key_ref)):
        cols = ref[...].astype(F32) * gain
        parts = [cols[:, j : j + HALF] for start in (0, HALF) for j in range(start, width, HEAD_DIM)]
        out_ref[:, i * width : (i + 1) * width] = jnp.concatenate(parts, axis=1).astype(BF)
    out_ref[:, 2 * width :] = (value_ref[...].astype(F32) * gain).astype(BF)


def qkv_out(parts, gain, *ws):
    own, full = ws[0].shape
    width = full // parts
    return pl.pallas_call(
        qkv_out_kernel,
        out_shape=jax.ShapeDtypeStruct((parts, own, 3 * width), BF),
        grid=(parts,),
        in_specs=[pl.BlockSpec((own, 1), lambda t: (0, 0))] + [pl.BlockSpec((own, width), lambda t: (0, t))] * 3,
        out_specs=pl.BlockSpec((None, own, 3 * width), lambda t: (t, 0, 0)),
        cost_estimate=pl.CostEstimate(flops=1, bytes_accessed=12 * ws[0].size, transcendentals=0),
        name="qkv_out",
    )(gain, *ws)


def qkv_back_kernel(gain_ref, hat_ref, query_ref, key_ref, value_ref, query_out, key_out, value_out, sum_ref):
    width = query_ref.shape[1]
    gain = gain_ref[...]
    total = jnp.zeros(gain.shape, F32)
    for i, (ref, out) in enumerate(((query_ref, query_out), (key_ref, key_out), (value_ref, value_out))):
        hat = hat_ref[:, i * width : (i + 1) * width].astype(F32)
        if i < 2:
            parts = [hat[:, j : j + HALF] for at in range(0, width // 2, HALF) for j in (at, width // 2 + at)]
            hat = jnp.concatenate(parts, axis=1)
        total += jnp.sum(hat * ref[...].astype(F32), axis=1, keepdims=True)
        out[...] = hat * gain

    @pl.when(pl.program_id(0) == 0)
    def _():
        sum_ref[...] = total

    @pl.when(pl.program_id(0) > 0)
    def _():
        sum_ref[...] += total


def qkv_back(gain, hat, *ws):
    own, full = ws[0].shape
    parts = hat.shape[0]
    width = full // parts
    part = pl.BlockSpec((own, width), lambda t: (0, t))
    column = pl.BlockSpec((own, 1), lambda t: (0, 0))
    return pl.pallas_call(
        qkv_back_kernel,
        out_shape=(jax.ShapeDtypeStruct((own, full), F32),) * 3 + (jax.ShapeDtypeStruct((own, 1), F32),),
        grid=(parts,),
        in_specs=[column, pl.BlockSpec((None, own, 3 * width), lambda t: (t, 0, 0)), part, part, part],
        out_specs=(part, part, part, column),
        cost_estimate=pl.CostEstimate(flops=1, bytes_accessed=24 * ws[0].size, transcendentals=0),
        name="qkv_back",
    )(gain, hat, *ws)


def after(value, *others):
    return lax.optimization_barrier((value, *others))[0] if others else value


def unit(values):
    inverse = lax.rsqrt(jnp.mean(values * values, axis=1, keepdims=True) + EPS)
    return values * inverse, inverse


def unit_back(grad, normed, inverse):
    return inverse * (grad - normed * jnp.mean(grad * normed, axis=1, keepdims=True))


def local(ring, plane, pair, inputs, norm1_gain, w_query, w_key, w_value, w_output, norm2_gain, w_gate, w_up, w_down, out_grad):
    seq_count, rows, model = inputs.shape
    parts = ring * pair
    own = w_query.shape[0]
    ff_own = w_down.shape[0]
    width = model // parts
    heads = width // HEAD_DIM
    half = width // 2
    ff = plane * ff_own
    group = ("seq", "core")
    z = lax.axis_index("seq")
    c = lax.axis_index("core")
    where = jnp.stack([z, c]).astype(jnp.int32)
    ring_pairs = [(i, (i + 1) % ring) for i in range(ring)]
    core_pairs = [(i, (i + 1) % pair) for i in range(pair)]

    def hop(x):
        return lax.ppermute(x, "seq", ring_pairs)

    def swap(x):
        return lax.ppermute(x, "core", core_pairs)

    def ring_sum(shares, *fill):
        total = shares[1].astype(BF)
        for k in range(2, ring):
            total = (hop(total).astype(F32) + shares[k]).astype(BF)
            total = after(total, *fill[k - 2 : k - 1])
        return hop(total).astype(F32) + shares[0]

    def both_cores(term):
        return term[0].astype(F32) + swap(term[1]).astype(F32)

    def exchange(x):
        return lax.all_to_all(x, group, 0, 0, tiled=True)

    def exchange_rows(x):
        return exchange(x).reshape(ring, pair * own, x.shape[2])

    def gather_rows(x):
        return lax.all_gather(x, "yx", axis=1, tiled=True).reshape(model, x.shape[2])

    def sum_rows(x):
        x = x.reshape(ring, plane * pair * own, x.shape[1])
        return lax.psum_scatter(x, "yx", scatter_dimension=1, tiled=True)

    def return_rows(x):
        return exchange(x.reshape(parts, own, x.shape[2]))

    gain_one, gain_two = norm1_gain.astype(F32)[:, None], norm2_gain.astype(F32)[:, None]

    residual = inputs.reshape(rows, model).astype(F32)
    normed_one, inverse_one = unit(residual)
    one = normed_one.astype(BF)
    qkv_w = qkv_out(parts, gain_one, w_query, w_key, w_value)
    ff_w = ff_out(ring, pair, ff_own, gain_two, w_gate, w_up)
    down_w = lax.all_gather(w_down, "yx", axis=0, tiled=True)
    ones = [one, hop(one)]
    qkv_w = exchange_rows(after(qkv_w, ones[1]))
    for k in range(1, ring - 1):
        ones.append(hop(after(ones[k], qkv_w if k == 1 else ff_w)))
    qkv_w = gather_rows(after(qkv_w, down_w))
    ff_w = exchange_rows(after(ff_w, ones[-1]))
    output_w = lax.all_gather(after(w_output, ones[1]), ("seq", "yx", "core"), axis=0, tiled=True)

    freqs = jnp.exp(jnp.arange(HALF, dtype=F32) * (-2.0 * math.log(ROPE_BASE) / HEAD_DIM))
    angle = jnp.arange(ring * rows, dtype=jnp.int32).astype(F32)[:, None] * freqs[None, :]
    cosine, sine = jnp.tile(jnp.cos(angle), (1, heads)), jnp.tile(jnp.sin(angle), (1, heads))
    kept = []
    for k in range(ring):
        kept = project(k, ring, kept, where, ones[k], swap(ones[k]), qkv_w, cosine, sine)
    all_ones, qkv = kept
    att_send, lse = attend(qkv, where, heads)
    att_send, ff_w = lax.optimization_barrier((att_send, ff_w))
    ff_w = gather_rows(ff_w)
    att = exchange(att_send).transpose(1, 0, 2).reshape(rows, model)
    mid = residual + mm(att, output_w)

    normed_two, inverse_two = unit(mid)
    twos = [normed_two.astype(BF)]
    grad_out = out_grad.reshape(rows, model)
    douts = [grad_out, hop(after(grad_out, att))]
    for k in range(1, ring):
        twos.append(hop(twos[-1]))
        if k < ring - 1:
            douts.append(hop(after(douts[-1], att if k == 1 else twos[k - 1])))
    kept, out_terms = [], [None] * ring
    for k in [1, 0, *range(2, ring)]:
        if k == 2:
            total = first_share
        two = after(twos[k], total) if k > 1 else twos[k]
        kept, out_terms[k], back = feed(k, ring, kept, two, swap(twos[k]), douts[k], swap(douts[k]), ff_w, down_w, ff_own)
        if k == 0:
            own_share = both_cores(back)
        elif k == 1:
            first_share = both_cores(back).astype(BF)
        else:
            here = hop(total).astype(F32) + back[0].astype(F32)
            if k == ring - 1:
                all_twos, all_douts, hiddens, dffs = kept
                ff_grad = mm_tn(after(all_twos, total), dffs).astype(BF)
                here = after(here, ff_grad)
            else:
                here = after(here, own_share)
            total = (here + swap(back[1]).astype(F32)).astype(BF)
    tokens = ring * pair * rows
    ff_grad = sum_rows(after(ff_grad, total))
    down_grad = mm_tn(hiddens, after(all_douts, total)).astype(BF)
    grad_two = after(hop(total).astype(F32) + own_share, down_grad)

    grad_mid = grad_out.astype(F32) + unit_back(grad_two, normed_two, inverse_two)
    proj = grad_mid.astype(BF)
    datt = mm_nt(proj, output_w).astype(BF)
    shares = [both_cores(after(t, grad_two)) for t in out_terms]
    total = (hop(shares[1].astype(BF)).astype(F32) + shares[2]).astype(BF)
    datt = datt.reshape(rows, parts, width).transpose(1, 0, 2)

    split = model // pair
    mine = lax.dynamic_slice_in_dim(att, c * split, split, axis=1)
    others = swap(lax.dynamic_slice_in_dim(att, (pair - 1 - c) * split, split, axis=1))
    output_grad = mm_tn(jnp.concatenate([mine, others]), jnp.concatenate([proj, swap(proj)])).astype(BF)
    datt = after(exchange(after(datt, total)), output_grad)
    output_grad = lax.psum_scatter(output_grad, "yx", scatter_dimension=0, tiled=True)
    dqkv = attend_back(qkv, datt, lse, cosine, sine, where, heads)
    total = after(total, datt)
    for k in range(3, ring):
        total = (hop(total).astype(F32) + shares[k]).astype(BF)
    dqkv = after(dqkv, ff_grad, total)
    output = (mid + (hop(total).astype(F32) + shares[0])).astype(BF).reshape(inputs.shape)
    ff_grad = return_rows(ff_grad)
    gate_grad, up_grad, gain_two_grad = ff_back(ring, ff_own, gain_two, ff_grad, w_gate, w_up)

    qkv_grad = mm_tn(all_ones, dqkv.reshape(tokens, 3 * width)).astype(BF)
    dqkv = after(dqkv, qkv_grad)
    down_grad = lax.psum_scatter(after(down_grad, qkv_grad), "yx", scatter_dimension=0, tiled=True).astype(F32)
    qkv_grad = sum_rows(qkv_grad)
    one_terms = [[mm_nt(dqkv[k, i], qkv_w).astype(BF) for i in range(pair)] for k in range(ring)]
    shares = [both_cores(t) for t in one_terms]
    total = after(shares[1].astype(BF), output, ff_grad)
    qkv_grad = return_rows(after(qkv_grad, output))
    total = after((hop(total).astype(F32) + shares[2]).astype(BF), qkv_grad)
    output_grad = after(output_grad, total)
    output_grad = output_grad.reshape(ring, own, model)
    output_grad = ring_sum(
        [lax.dynamic_index_in_dim(output_grad, lax.rem(z - k + ring, ring), keepdims=False).astype(F32) for k in range(ring)]
    ).astype(BF)
    moves = [((s * plane + y) * pair + h, (h * plane + y) * ring + s) for s in range(ring) for y in range(plane) for h in range(pair)]
    output_grad = lax.ppermute(output_grad, ("seq", "yx", "core"), moves).astype(F32)

    query_grad, key_grad, value_grad, gain_one_grad = qkv_back(gain_one, qkv_grad, w_query, w_key, w_value)
    for k in range(3, ring):
        total = (hop(total).astype(F32) + shares[k]).astype(BF)
    total = after(total, qkv_grad)
    total, gate_grad, up_grad, gain_two_grad, output_grad = lax.optimization_barrier(
        (total, gate_grad, up_grad, gain_two_grad, output_grad)
    )
    grad_one = hop(total).astype(F32) + shares[0]
    input_grad = (grad_mid + unit_back(grad_one, normed_one, inverse_one)).reshape(inputs.shape)
    return (
        output,
        input_grad,
        gain_one_grad[:, 0],
        query_grad,
        key_grad,
        value_grad,
        output_grad,
        gain_two_grad[:, 0],
        gate_grad,
        up_grad,
        down_grad,
    )


def solution(mesh):
    ring, fsdp = mesh.shape["seq"], mesh.shape["fsdp"]
    pair = 2
    plane = fsdp // pair
    fine = Mesh(mesh.devices.reshape(ring, plane, pair), ("seq", "yx", "core"))
    tokens = P(("yx", "core"), "seq", None)
    every = ("seq", "yx", "core")
    weight, gain = P(every, None), P(every)
    return jax.shard_map(
        functools.partial(local, ring, plane, pair),
        mesh=fine,
        in_specs=(tokens, gain, weight, weight, weight, weight, gain, weight, weight, weight, tokens),
        out_specs=(tokens, tokens, gain, weight, weight, weight, weight, gain, weight, weight, weight),
        check_vma=False,
    )
```

```python
import functools
import math

import jax
import jax.numpy as jnp
from jax import lax
from jax.experimental import pallas as pl
from jax.experimental.pallas import tpu as pltpu
from jax.sharding import Mesh
from jax.sharding import PartitionSpec as P

HEAD_DIM = 64
HALF = HEAD_DIM // 2
SCALE = HEAD_DIM ** (-0.5)
EPS = 1e-05
ROPE_BASE = 130000.0
BF = jnp.bfloat16
F32 = jnp.float32
QUICK = pl.CostEstimate(flops=1, bytes_accessed=1, transcendentals=0)


def dot(left, right, dims):
    return lax.dot_general(left, right, (dims, ((), ())), preferred_element_type=F32)


def mm(left, right):
    return dot(left, right, ((left.ndim - 1,), (0,)))


def mm_nt(left, right):
    return dot(left, right, ((left.ndim - 1,), (1,)))


def mm_tn(left, right):
    return dot(left, right, ((0,), (0,)))


def qk_head(width, head):
    lane = lax.broadcasted_iota(jnp.int32, (1, width), 1)
    return (lane % (width // 2)) // HALF == head


def v_head(width, head):
    return lax.broadcasted_iota(jnp.int32, (1, width), 1) // HEAD_DIM == head


def causal(rows):
    key = lax.broadcasted_iota(jnp.int32, (rows, rows), 0)
    query = lax.broadcasted_iota(jnp.int32, (rows, rows), 1)
    return key <= query


def attend_kernel(heads, ring, where_ref, qkv_ref, send_ref, lse_ref, key_ref, vt_ref, ot_ref):
    rows, width = qkv_ref.shape[1], qkv_ref.shape[2] // 3
    block = pl.program_id(1)
    z = where_ref[0]

    @pl.when(block == 0)
    def _():
        for p in range(ring):
            at = lax.rem(z - p + ring, ring)
            key_ref[p * rows : (p + 1) * rows] = qkv_ref[at, :, width : 2 * width]
            vt_ref[:, p * rows : (p + 1) * rows] = qkv_ref[at, :, 2 * width :].T

    def one(p):
        done = p * rows
        query = qkv_ref[lax.rem(z - p + ring, ring), :, :width]
        keep = causal(rows)
        for head in range(heads):
            query_h = jnp.where(qk_head(width, head), query, jnp.zeros_like(query))
            diag = dot(key_ref[done : done + rows], query_h, ((1,), (1,))) * SCALE
            diag = jnp.where(keep, diag, -1e30)
            top = jnp.max(diag, axis=0, keepdims=True)
            if p:
                past = dot(key_ref[:done], query_h, ((1,), (1,))) * SCALE
                top = jnp.maximum(top, jnp.max(past, axis=0, keepdims=True))
                past = jnp.exp(past - top)
            diag = jnp.exp(diag - top)
            total = jnp.sum(diag, axis=0, keepdims=True)
            if p:
                total = total + jnp.sum(past, axis=0, keepdims=True)
            share = 1.0 / total
            at = slice(head * HEAD_DIM, (head + 1) * HEAD_DIM)
            out = mm(vt_ref[at, done : done + rows], (diag * share).astype(BF))
            if p:
                out = out + mm(vt_ref[at, :done], (past * share).astype(BF))
            ot_ref[at] = out
            lse_ref[head : head + 1] = top + jnp.log(total)
        send_ref[...] = ot_ref[...].T.astype(BF)

    for p in range(ring):
        pl.when(block == p)(functools.partial(one, p))


def attend(qkv, where, heads):
    ring, pair, rows, full = qkv.shape
    width = full // 3
    return pl.pallas_call(
        functools.partial(attend_kernel, heads, ring),
        out_shape=(
            jax.ShapeDtypeStruct((ring * pair, rows, width), BF),
            jax.ShapeDtypeStruct((pair, ring, heads, rows), F32),
        ),
        grid_spec=pltpu.PrefetchScalarGridSpec(
            num_scalar_prefetch=1,
            grid=(pair, ring),
            in_specs=[pl.BlockSpec((ring, None, rows, full), lambda i, p, w: (0, i, 0, 0))],
            out_specs=[
                pl.BlockSpec((None, rows, width), lambda i, p, w: (p * pair + lax.rem(w[1] + i, pair), 0, 0)),
                pl.BlockSpec((None, None, heads, rows), lambda i, p, w: (i, p, 0, 0)),
            ],
            scratch_shapes=[
                pltpu.VMEM((ring * rows, width), BF),
                pltpu.VMEM((width, ring * rows), BF),
                pltpu.VMEM((width, rows), F32),
            ],
        ),
        compiler_params=pltpu.CompilerParams(vmem_limit_bytes=48 << 20),
        cost_estimate=pl.CostEstimate(flops=20 * 10**9, bytes_accessed=2 * qkv.size * 2, transcendentals=0),
        name="attend",
    )(where, qkv)


def attend_back_kernel(
    heads, ring, where_ref, qkv_ref, datt_ref, lse_ref, cos_ref, sin_ref, out_ref,
    key_ref, kt_ref, val_ref, qt_ref, dk_ref, dv_ref,
):
    rows, width = qkv_ref.shape[1], qkv_ref.shape[2] // 3
    half = width // 2
    block = pl.program_id(1)
    z = where_ref[0]

    @pl.when(block == 0)
    def _():
        for p in range(ring):
            at = lax.rem(z - p + ring, ring)
            key = qkv_ref[at, :, width : 2 * width]
            key_ref[p * rows : (p + 1) * rows] = key
            kt_ref[:, p * rows : (p + 1) * rows] = key.T
            val_ref[p * rows : (p + 1) * rows] = qkv_ref[at, :, 2 * width :]
        dk_ref[...] = jnp.zeros_like(dk_ref)
        dv_ref[...] = jnp.zeros_like(dv_ref)

    def turn_back(grad, p):
        cosine, sine = cos_ref[p * rows : (p + 1) * rows], sin_ref[p * rows : (p + 1) * rows]
        grad = grad.astype(BF).astype(F32)
        first, second = grad[:, :half], grad[:, half:]
        return (first * cosine + second * sine).astype(BF), (second * cosine - first * sine).astype(BF)

    def one(p):
        done = p * rows
        at = lax.rem(z - p + ring, ring)
        query = qkv_ref[at, :, :width]
        grad = datt_ref[...]
        keep = causal(rows)
        for head in range(heads):
            query_h = jnp.where(qk_head(width, head), query, jnp.zeros_like(query))
            grad_h = jnp.where(v_head(width, head), grad, jnp.zeros_like(grad))
            lse = lse_ref[head : head + 1]
            parts = []
            for low, high in ([(0, done)] if p else []) + [(done, done + rows)]:
                score = dot(key_ref[low:high], query_h, ((1,), (1,))) * SCALE
                prob = jnp.exp(score - lse)
                if low == done:
                    prob = jnp.where(keep, prob, 0.0)
                dprob = dot(val_ref[low:high], grad_h, ((1,), (1,)))
                parts.append((low, high, prob, dprob))
            delta = sum(jnp.sum(prob * dprob, axis=0, keepdims=True) for _, _, prob, dprob in parts)
            turned = 0.0
            for low, high, prob, dprob in parts:
                dscore = (prob * (dprob - delta)).astype(BF)
                key_t = jnp.concatenate(
                    [
                        kt_ref[head * HALF : (head + 1) * HALF, low:high],
                        kt_ref[half + head * HALF : half + (head + 1) * HALF, low:high],
                    ],
                    axis=0,
                )
                turned = turned + mm(key_t, dscore)
                dk_ref[low:high] += mm(dscore, query_h)
                dv_ref[low:high] += mm(prob.astype(BF), grad_h)
            qt_ref[head * HALF : (head + 1) * HALF] = turned[:HALF]
            qt_ref[half + head * HALF : half + (head + 1) * HALF] = turned[HALF:]
        first, second = turn_back(qt_ref[...].T * SCALE, p)
        out_ref[at, :, :half] = first
        out_ref[at, :, half:width] = second

    for p in range(ring):
        pl.when(block == p)(functools.partial(one, p))

    @pl.when(block == ring - 1)
    def _():
        for p in range(ring):
            at = lax.rem(z - p + ring, ring)
            first, second = turn_back(dk_ref[p * rows : (p + 1) * rows] * SCALE, p)
            out_ref[at, :, width : width + half] = first
            out_ref[at, :, width + half : 2 * width] = second
            out_ref[at, :, 2 * width :] = dv_ref[p * rows : (p + 1) * rows].astype(BF)


def attend_back(qkv, datt, lse, cosine, sine, where, heads):
    ring, pair, rows, full = qkv.shape
    width = full // 3
    return pl.pallas_call(
        functools.partial(attend_back_kernel, heads, ring),
        out_shape=jax.ShapeDtypeStruct(qkv.shape, BF),
        grid_spec=pltpu.PrefetchScalarGridSpec(
            num_scalar_prefetch=1,
            grid=(pair, ring),
            in_specs=[
                pl.BlockSpec((ring, None, rows, full), lambda i, p, w: (0, i, 0, 0)),
                pl.BlockSpec((None, rows, width), lambda i, p, w: (p * pair + lax.rem(w[1] + i, pair), 0, 0)),
                pl.BlockSpec((None, None, heads, rows), lambda i, p, w: (i, p, 0, 0)),
                pl.BlockSpec((ring * rows, width // 2), lambda i, p, w: (0, 0)),
                pl.BlockSpec((ring * rows, width // 2), lambda i, p, w: (0, 0)),
            ],
            out_specs=pl.BlockSpec((ring, None, rows, full), lambda i, p, w: (0, i, 0, 0)),
            scratch_shapes=[
                pltpu.VMEM((ring * rows, width), BF),
                pltpu.VMEM((width, ring * rows), BF),
                pltpu.VMEM((ring * rows, width), BF),
                pltpu.VMEM((width, rows), F32),
                pltpu.VMEM((ring * rows, width), F32),
                pltpu.VMEM((ring * rows, width), F32),
            ],
        ),
        compiler_params=pltpu.CompilerParams(vmem_limit_bytes=52 << 20),
        cost_estimate=pl.CostEstimate(flops=28 * 10**9, bytes_accessed=4 * qkv.size * 2, transcendentals=0),
        name="attend_back",
    )(where, qkv, datt, lse, cosine, sine)


def feed_kernel(
    steps, two_ref, two_other_ref, dout_ref, dout_other_ref, ff_in_ref, down_in_ref, ff_back_ref, down_out_ref, *refs,
):
    x_ref, dy_ref, hidden_ref, dff_ref, out_ref, out_other_ref, back_ref, back_other_ref = refs[-8:]
    rows = two_ref.shape[0]
    chunk = down_in_ref.shape[0]
    step = pl.program_id(0)

    @pl.when(step == 0)
    def _():
        x_ref[:rows], x_ref[rows:] = two_ref[...], two_other_ref[...]
        dy_ref[:rows], dy_ref[rows:] = dout_ref[...], dout_other_ref[...]

    def hidden_units(j):
        both = mm(x_ref[...], ff_in_ref[...])
        dhid = mm_nt(dy_ref[...], down_in_ref[...])
        gate, up = both[:, :chunk], both[:, chunk:]
        sig = jax.nn.sigmoid(gate)
        act = gate * sig
        hidden_ref[:, j * chunk : (j + 1) * chunk] = (act * up).astype(BF)
        dgate = dhid * up * (sig * (1.0 + gate * (1.0 - sig)))
        dff_ref[:, 2 * j * chunk : (2 * j + 1) * chunk] = dgate.astype(BF)
        dff_ref[:, (2 * j + 1) * chunk : (2 * j + 2) * chunk] = (dhid * act).astype(BF)

    for j in range(steps):
        pl.when(step == j)(functools.partial(hidden_units, j))

    @pl.when(step >= steps)
    def _():
        out = mm(hidden_ref[...], down_out_ref[...]).astype(BF)
        out_ref[...], out_other_ref[...] = out[:rows], out[rows:]
        back = mm_nt(dff_ref[...], ff_back_ref[...]).astype(BF)
        back_ref[...], back_other_ref[...] = back[:rows], back[rows:]


def feed(k, blocks, kept, two, two_other, dout, dout_other, ff_w, down_w, chunk):
    rows, model = two.shape
    ff = down_w.shape[0]
    steps = ff // chunk
    part = model // steps
    whole = pl.BlockSpec((rows, model), lambda j: (0, 0))
    share = pl.BlockSpec((rows, part), lambda j: (0, jnp.maximum(j - steps, 0)))
    widths = (model, model, ff, 2 * ff)
    *kept, out, out_other, back, back_other = pl.pallas_call(
        functools.partial(feed_kernel, steps),
        out_shape=[jax.ShapeDtypeStruct((blocks * 2 * rows, w), BF) for w in widths] + [jax.ShapeDtypeStruct((rows, model), BF)] * 4,
        grid=(2 * steps,),
        in_specs=[
            whole, whole, whole, whole,
            pl.BlockSpec((model, 2 * chunk), lambda j: (0, jnp.minimum(j, steps - 1))),
            pl.BlockSpec((chunk, model), lambda j: (jnp.minimum(j, steps - 1), 0)),
            pl.BlockSpec((part, 2 * ff), lambda j: (jnp.maximum(j - steps, 0), 0)),
            pl.BlockSpec((ff, part), lambda j: (0, jnp.maximum(j - steps, 0))),
        ] + [pl.BlockSpec(memory_space=pl.ANY)] * len(kept),
        out_specs=[pl.BlockSpec((2 * rows, w), lambda j: (k, 0)) for w in widths] + [share] * 4,
        input_output_aliases={8 + i: i for i in range(len(kept))},
        compiler_params=pltpu.CompilerParams(vmem_limit_bytes=56 << 20),
        cost_estimate=pl.CostEstimate(flops=2 * rows * model * ff * 6 // 4, bytes_accessed=1, transcendentals=0),
        name="feed",
    )(two, two_other, dout, dout_other, ff_w, down_w, ff_w, down_w, *kept)
    return kept, (out, out_other), (back, back_other)


def project_kernel(where_ref, one_ref, other_ref, w_ref, cos_ref, sin_ref, *refs):
    x_ref, out_ref = refs[-2:]
    rows = one_ref.shape[0]
    half = w_ref.shape[1] // 2
    step = pl.program_id(0)

    @pl.when(step == 0)
    def _():
        x_ref[:rows], x_ref[rows:] = one_ref[...], other_ref[...]

    flat = mm(x_ref[...], w_ref[...])

    @pl.when(step < 2)
    def _():
        cosine, sine = cos_ref[...], sin_ref[...]
        for i in range(2):
            first, second = flat[i * rows : (i + 1) * rows, :half], flat[i * rows : (i + 1) * rows, half:]
            out_ref[i, :, :half] = (first * cosine - second * sine).astype(BF)
            out_ref[i, :, half:] = (second * cosine + first * sine).astype(BF)

    @pl.when(step == 2)
    def _():
        out_ref[0], out_ref[1] = flat[:rows].astype(BF), flat[rows:].astype(BF)


def project(k, blocks, kept, where, one, other, w, cosine, sine):
    rows, model = cosine.shape[0] // blocks, one.shape[1]
    width = w.shape[1] // 3
    whole = pl.BlockSpec((rows, model), lambda j, at: (0, 0))
    table = pl.BlockSpec((rows, width // 2), lambda j, at: (lax.rem(at[0] - k + blocks, blocks), 0))
    return pl.pallas_call(
        project_kernel,
        out_shape=(
            jax.ShapeDtypeStruct((blocks * 2 * rows, model), BF),
            jax.ShapeDtypeStruct((blocks, 2, rows, 3 * width), BF),
        ),
        grid_spec=pltpu.PrefetchScalarGridSpec(
            num_scalar_prefetch=1,
            grid=(3,),
            in_specs=[whole, whole, pl.BlockSpec((model, width), lambda j, at: (0, j)), table, table]
            + [pl.BlockSpec(memory_space=pl.ANY)] * len(kept),
            out_specs=(
                pl.BlockSpec((2 * rows, model), lambda j, at: (k, 0)),
                pl.BlockSpec((None, 2, rows, width), lambda j, at: (k, 0, 0, j)),
            ),
        ),
        input_output_aliases={6 + i: i for i in range(len(kept))},
        compiler_params=pltpu.CompilerParams(vmem_limit_bytes=40 << 20),
        cost_estimate=QUICK,
        name="project",
    )(where, one, other, w, cosine, sine, *kept)


def ff_out_kernel(turn, gain_ref, gate_ref, up_ref, out_ref):
    pair = out_ref.shape[0]
    gain = gain_ref[...]
    for y in range(out_ref.shape[2] // (2 * turn)):
        for c in range(pair):
            at = (y * pair + c) * turn
            for i, ref in enumerate((gate_ref, up_ref)):
                cols = (ref[:, at : at + turn].astype(F32) * gain).astype(BF)
                out_ref[c, :, (2 * y + i) * turn : (2 * y + i + 1) * turn] = cols


def ff_out(ring, pair, turn, gain, w_gate, w_up):
    own, full = w_gate.shape
    part = pl.BlockSpec((own, full // ring), lambda s: (0, s))
    return pl.pallas_call(
        functools.partial(ff_out_kernel, turn),
        out_shape=jax.ShapeDtypeStruct((ring * pair, own, 2 * full // (ring * pair)), BF),
        grid=(ring,),
        in_specs=[pl.BlockSpec((own, 1), lambda s: (0, 0)), part, part],
        out_specs=pl.BlockSpec((pair, own, 2 * full // (ring * pair)), lambda s: (s, 0, 0)),
        cost_estimate=pl.CostEstimate(flops=1, bytes_accessed=8 * w_gate.size, transcendentals=0),
        name="ff_out",
    )(gain, w_gate, w_up)


def ff_back_kernel(turn, gain_ref, hat_ref, gate_ref, up_ref, gate_out, up_out, sum_ref):
    pair = hat_ref.shape[0]
    gain = gain_ref[...]
    total = jnp.zeros(gain.shape, F32)
    for y in range(hat_ref.shape[2] // (2 * turn)):
        for c in range(pair):
            at = (y * pair + c) * turn
            for i, (ref, out) in enumerate(((gate_ref, gate_out), (up_ref, up_out))):
                hat = hat_ref[c, :, (2 * y + i) * turn : (2 * y + i + 1) * turn].astype(F32)
                total += jnp.sum(hat * ref[:, at : at + turn].astype(F32), axis=1, keepdims=True)
                out[:, at : at + turn] = hat * gain

    @pl.when(pl.program_id(0) == 0)
    def _():
        sum_ref[...] = total

    @pl.when(pl.program_id(0) > 0)
    def _():
        sum_ref[...] += total


def ff_back(ring, turn, gain, hat, w_gate, w_up):
    own, full = w_gate.shape
    pair = hat.shape[0] // ring
    part = pl.BlockSpec((own, full // ring), lambda s: (0, s))
    column = pl.BlockSpec((own, 1), lambda s: (0, 0))
    return pl.pallas_call(
        functools.partial(ff_back_kernel, turn),
        out_shape=(jax.ShapeDtypeStruct((own, full), F32),) * 2 + (jax.ShapeDtypeStruct((own, 1), F32),),
        grid=(ring,),
        in_specs=[column, pl.BlockSpec((pair, *hat.shape[1:]), lambda s: (s, 0, 0)), part, part],
        out_specs=(part, part, column),
        cost_estimate=pl.CostEstimate(flops=1, bytes_accessed=16 * w_gate.size, transcendentals=0),
        name="ff_back",
    )(gain, hat, w_gate, w_up)


def qkv_out_kernel(gain_ref, query_ref, key_ref, value_ref, out_ref):
    width = query_ref.shape[1]
    gain = gain_ref[...]
    for i, ref in enumerate((query_ref, key_ref)):
        cols = ref[...].astype(F32) * gain
        parts = [cols[:, j : j + HALF] for start in (0, HALF) for j in range(start, width, HEAD_DIM)]
        out_ref[:, i * width : (i + 1) * width] = jnp.concatenate(parts, axis=1).astype(BF)
    out_ref[:, 2 * width :] = (value_ref[...].astype(F32) * gain).astype(BF)


def qkv_out(parts, gain, *ws):
    own, full = ws[0].shape
    width = full // parts
    return pl.pallas_call(
        qkv_out_kernel,
        out_shape=jax.ShapeDtypeStruct((parts, own, 3 * width), BF),
        grid=(parts,),
        in_specs=[pl.BlockSpec((own, 1), lambda t: (0, 0))] + [pl.BlockSpec((own, width), lambda t: (0, t))] * 3,
        out_specs=pl.BlockSpec((None, own, 3 * width), lambda t: (t, 0, 0)),
        cost_estimate=pl.CostEstimate(flops=1, bytes_accessed=12 * ws[0].size, transcendentals=0),
        name="qkv_out",
    )(gain, *ws)


def qkv_back_kernel(gain_ref, hat_ref, query_ref, key_ref, value_ref, query_out, key_out, value_out, sum_ref):
    width = query_ref.shape[1]
    gain = gain_ref[...]
    total = jnp.zeros(gain.shape, F32)
    for i, (ref, out) in enumerate(((query_ref, query_out), (key_ref, key_out), (value_ref, value_out))):
        hat = hat_ref[:, i * width : (i + 1) * width].astype(F32)
        if i < 2:
            parts = [hat[:, j : j + HALF] for at in range(0, width // 2, HALF) for j in (at, width // 2 + at)]
            hat = jnp.concatenate(parts, axis=1)
        total += jnp.sum(hat * ref[...].astype(F32), axis=1, keepdims=True)
        out[...] = hat * gain

    @pl.when(pl.program_id(0) == 0)
    def _():
        sum_ref[...] = total

    @pl.when(pl.program_id(0) > 0)
    def _():
        sum_ref[...] += total


def qkv_back(gain, hat, *ws):
    own, full = ws[0].shape
    parts = hat.shape[0]
    width = full // parts
    part = pl.BlockSpec((own, width), lambda t: (0, t))
    column = pl.BlockSpec((own, 1), lambda t: (0, 0))
    return pl.pallas_call(
        qkv_back_kernel,
        out_shape=(jax.ShapeDtypeStruct((own, full), F32),) * 3 + (jax.ShapeDtypeStruct((own, 1), F32),),
        grid=(parts,),
        in_specs=[column, pl.BlockSpec((None, own, 3 * width), lambda t: (t, 0, 0)), part, part, part],
        out_specs=(part, part, part, column),
        cost_estimate=pl.CostEstimate(flops=1, bytes_accessed=24 * ws[0].size, transcendentals=0),
        name="qkv_back",
    )(gain, hat, *ws)


def after(value, *others):
    return lax.optimization_barrier((value, *others))[0] if others else value


def unit(values):
    inverse = lax.rsqrt(jnp.mean(values * values, axis=1, keepdims=True) + EPS)
    return values * inverse, inverse


def unit_back(grad, normed, inverse):
    return inverse * (grad - normed * jnp.mean(grad * normed, axis=1, keepdims=True))


def local(ring, plane, pair, inputs, norm1_gain, w_query, w_key, w_value, w_output, norm2_gain, w_gate, w_up, w_down, out_grad):
    seq_count, rows, model = inputs.shape
    parts = ring * pair
    own = w_query.shape[0]
    ff_own = w_down.shape[0]
    width = model // parts
    heads = width // HEAD_DIM
    half = width // 2
    ff = plane * ff_own
    group = ("seq", "core")
    z = lax.axis_index("seq")
    c = lax.axis_index("core")
    where = jnp.stack([z, c]).astype(jnp.int32)
    ring_pairs = [(i, (i + 1) % ring) for i in range(ring)]
    core_pairs = [(i, (i + 1) % pair) for i in range(pair)]

    def hop(x):
        return lax.ppermute(x, "seq", ring_pairs)

    def swap(x):
        return lax.ppermute(x, "core", core_pairs)

    def ring_sum(shares, *fill):
        total = shares[1].astype(BF)
        for k in range(2, ring):
            total = (hop(total).astype(F32) + shares[k]).astype(BF)
            total = after(total, *fill[k - 2 : k - 1])
        return hop(total).astype(F32) + shares[0]

    def both_cores(term):
        return term[0].astype(F32) + swap(term[1]).astype(F32)

    def exchange(x):
        return lax.all_to_all(x, group, 0, 0, tiled=True)

    def exchange_rows(x):
        return exchange(x).reshape(ring, pair * own, x.shape[2])

    def gather_rows(x):
        return lax.all_gather(x, "yx", axis=1, tiled=True).reshape(model, x.shape[2])

    def sum_rows(x):
        x = x.reshape(ring, plane * pair * own, x.shape[1])
        return lax.psum_scatter(x, "yx", scatter_dimension=1, tiled=True)

    def return_rows(x):
        return exchange(x.reshape(parts, own, x.shape[2]))

    gain_one, gain_two = norm1_gain.astype(F32)[:, None], norm2_gain.astype(F32)[:, None]

    residual = inputs.reshape(rows, model).astype(F32)
    normed_one, inverse_one = unit(residual)
    one = jnp.concatenate([normed_one.astype(BF), w_output])
    qkv_w = qkv_out(parts, gain_one, w_query, w_key, w_value)
    ff_w = ff_out(ring, pair, ff_own, gain_two, w_gate, w_up)
    down_w = lax.all_gather(w_down, "yx", axis=0, tiled=True)
    ones = [one, hop(one)]
    qkv_w = exchange_rows(after(qkv_w, ones[1]))
    qkv_sent, qkv_w = qkv_w, gather_rows(after(qkv_w, down_w))
    for k in range(1, ring - 1):
        ones.append(hop(after(ones[k], qkv_sent if k == 1 else ff_w, *([qkv_w] if k == ring - 2 else []))))
    ff_w = exchange_rows(after(ff_w, ones[-1], qkv_w))
    output_w = jnp.stack([ones[k][rows:] for k in reversed(range(ring))] * 2)
    output_w = lax.dynamic_slice_in_dim(output_w, ring - 1 - z, ring)
    output_w = lax.all_gather(output_w, ("yx", "core"), axis=1, tiled=True).reshape(model, model)

    freqs = jnp.exp(jnp.arange(HALF, dtype=F32) * (-2.0 * math.log(ROPE_BASE) / HEAD_DIM))
    angle = jnp.arange(ring * rows, dtype=jnp.int32).astype(F32)[:, None] * freqs[None, :]
    cosine, sine = jnp.tile(jnp.cos(angle), (1, heads)), jnp.tile(jnp.sin(angle), (1, heads))
    kept = []
    for k in range(ring):
        kept = project(k, ring, kept, where, ones[k], swap(ones[k]), qkv_w, cosine, sine)
    all_ones, qkv = kept
    att_send, lse = attend(qkv, where, heads)
    att_send, ff_w = lax.optimization_barrier((att_send, ff_w))
    ff_w = gather_rows(ff_w)
    att = exchange(att_send).transpose(1, 0, 2).reshape(rows, model)
    mid = residual + mm(att, output_w)

    normed_two, inverse_two = unit(mid)
    twos = [normed_two.astype(BF)]
    grad_out = out_grad.reshape(rows, model)
    douts = [grad_out, hop(after(grad_out, att))]
    for k in range(1, ring):
        twos.append(hop(twos[-1]))
        if k < ring - 1:
            douts.append(hop(after(douts[-1], att if k == 1 else twos[k - 1])))
    kept, out_terms = [], [None] * ring
    for k in [1, 0, *range(2, ring)]:
        if k == 2:
            total = first_share
        two = after(twos[k], total) if k > 1 else twos[k]
        kept, out_terms[k], back = feed(k, ring, kept, two, swap(twos[k]), douts[k], swap(douts[k]), ff_w, down_w, ff_own)
        if k == 0:
            own_share = both_cores(back)
        elif k == 1:
            first_share = both_cores(back).astype(BF)
        else:
            here = hop(total).astype(F32) + back[0].astype(F32)
            here = after(here, own_share)
            total = (here + swap(back[1]).astype(F32)).astype(BF)
    tokens = ring * pair * rows
    all_twos, all_douts, hiddens, dffs = kept
    ff_grad = mm_tn(after(all_twos, total), dffs).astype(BF)
    grad_two = after(hop(total).astype(F32) + own_share, ff_grad)
    ff_grad = sum_rows(after(ff_grad, grad_two))

    grad_mid = grad_out.astype(F32) + unit_back(grad_two, normed_two, inverse_two)
    proj = grad_mid.astype(BF)
    datt = mm_nt(proj, output_w).astype(BF)
    datt = datt.reshape(rows, parts, width).transpose(1, 0, 2)

    split = model // pair
    mine = lax.dynamic_slice_in_dim(att, c * split, split, axis=1)
    others = swap(lax.dynamic_slice_in_dim(att, (pair - 1 - c) * split, split, axis=1))
    output_grad = mm_tn(jnp.concatenate([mine, others]), jnp.concatenate([proj, swap(proj)])).astype(BF)
    shares = [both_cores(after(t, grad_two)) for t in out_terms]
    total = (hop(shares[1].astype(BF)).astype(F32) + shares[2]).astype(BF)
    datt = after(exchange(datt), output_grad, total)
    dqkv = attend_back(qkv, datt, lse, cosine, sine, where, heads)
    total = after(total, datt)
    for k in range(3, ring):
        total = (hop(total).astype(F32) + shares[k]).astype(BF)
    dqkv = after(dqkv, ff_grad, total)
    output = (mid + (hop(total).astype(F32) + shares[0])).astype(BF).reshape(inputs.shape)
    ff_grad = return_rows(ff_grad)
    gate_grad, up_grad, gain_two_grad = ff_back(ring, ff_own, gain_two, ff_grad, w_gate, w_up)

    qkv_grad = mm_tn(all_ones, dqkv.reshape(tokens, 3 * width)).astype(BF)
    dqkv = after(dqkv, qkv_grad)
    down_grad = mm_tn(hiddens, after(all_douts, dqkv)).astype(BF)
    down_grad = lax.psum_scatter(down_grad, "yx", scatter_dimension=0, tiled=True).astype(F32)
    qkv_grad = sum_rows(qkv_grad)
    one_terms = [[mm_nt(dqkv[k, i], qkv_w).astype(BF) for i in range(pair)] for k in range(ring)]
    shares = [both_cores(t) for t in one_terms]
    total = (hop(shares[1].astype(BF)).astype(F32) + shares[2]).astype(BF)
    output_grad = lax.psum_scatter(after(output_grad, one_terms[1][0]), "yx", scatter_dimension=0, tiled=True)
    qkv_grad = return_rows(qkv_grad)
    total, qkv_grad, gate_grad, up_grad, gain_two_grad, output = lax.optimization_barrier(
        (total, qkv_grad, gate_grad, up_grad, gain_two_grad, output)
    )
    query_grad, key_grad, value_grad, gain_one_grad = qkv_back(gain_one, qkv_grad, w_query, w_key, w_value)
    for k in range(3, ring):
        total = (hop(total).astype(F32) + shares[k]).astype(BF)
    output_grad = after(output_grad, total).reshape(ring, own, model)
    output_grad = ring_sum(
        [lax.dynamic_index_in_dim(output_grad, lax.rem(z - k + ring, ring), keepdims=False).astype(F32) for k in range(ring)]
    ).astype(BF)
    moves = [((s * plane + y) * pair + h, (h * plane + y) * ring + s) for s in range(ring) for y in range(plane) for h in range(pair)]
    output_grad = lax.ppermute(output_grad, ("seq", "yx", "core"), moves).astype(F32)
    grad_one = hop(total).astype(F32) + shares[0]
    input_grad = (grad_mid + unit_back(grad_one, normed_one, inverse_one)).reshape(inputs.shape)
    return (
        output,
        input_grad,
        gain_one_grad[:, 0],
        query_grad,
        key_grad,
        value_grad,
        output_grad,
        gain_two_grad[:, 0],
        gate_grad,
        up_grad,
        down_grad,
    )


def solution(mesh):
    ring, fsdp = mesh.shape["seq"], mesh.shape["fsdp"]
    pair = 2
    plane = fsdp // pair
    fine = Mesh(mesh.devices.reshape(ring, plane, pair), ("seq", "yx", "core"))
    tokens = P(("yx", "core"), "seq", None)
    every = ("seq", "yx", "core")
    weight, gain = P(every, None), P(every)
    return jax.shard_map(
        functools.partial(local, ring, plane, pair),
        mesh=fine,
        in_specs=(tokens, gain, weight, weight, weight, weight, gain, weight, weight, weight, tokens),
        out_specs=(tokens, tokens, gain, weight, weight, weight, weight, gain, weight, weight, weight),
        check_vma=False,
    )
```

```python
import functools
import math

import jax
import jax.numpy as jnp
from jax import lax
from jax.experimental import pallas as pl
from jax.experimental.pallas import tpu as pltpu
from jax.sharding import Mesh
from jax.sharding import PartitionSpec as P

HEAD_DIM = 64
HALF = HEAD_DIM // 2
SCALE = HEAD_DIM ** (-0.5)
EPS = 1e-05
ROPE_BASE = 130000.0
BF = jnp.bfloat16
F32 = jnp.float32
QUICK = pl.CostEstimate(flops=1, bytes_accessed=1, transcendentals=0)


def dot(left, right, dims):
    return lax.dot_general(left, right, (dims, ((), ())), preferred_element_type=F32)


def mm(left, right):
    return dot(left, right, ((left.ndim - 1,), (0,)))


def mm_nt(left, right):
    return dot(left, right, ((left.ndim - 1,), (1,)))


def mm_tn(left, right):
    return dot(left, right, ((0,), (0,)))


def qk_head(width, head):
    lane = lax.broadcasted_iota(jnp.int32, (1, width), 1)
    return (lane % (width // 2)) // HALF == head


def v_head(width, head):
    return lax.broadcasted_iota(jnp.int32, (1, width), 1) // HEAD_DIM == head


def causal(rows):
    key = lax.broadcasted_iota(jnp.int32, (rows, rows), 0)
    query = lax.broadcasted_iota(jnp.int32, (rows, rows), 1)
    return key <= query


def attend_kernel(heads, ring, where_ref, qkv_ref, send_ref, lse_ref, key_ref, vt_ref, ot_ref):
    rows, width = qkv_ref.shape[1], qkv_ref.shape[2] // 3
    block = pl.program_id(1)
    z = where_ref[0]

    @pl.when(block == 0)
    def _():
        for p in range(ring):
            at = lax.rem(z - p + ring, ring)
            key_ref[p * rows : (p + 1) * rows] = qkv_ref[at, :, width : 2 * width]
            vt_ref[:, p * rows : (p + 1) * rows] = qkv_ref[at, :, 2 * width :].T

    def one(p):
        done = p * rows
        query = qkv_ref[lax.rem(z - p + ring, ring), :, :width]
        keep = causal(rows)
        for head in range(heads):
            query_h = jnp.where(qk_head(width, head), query, jnp.zeros_like(query))
            diag = dot(key_ref[done : done + rows], query_h, ((1,), (1,))) * SCALE
            diag = jnp.where(keep, diag, -1e30)
            top = jnp.max(diag, axis=0, keepdims=True)
            if p:
                past = dot(key_ref[:done], query_h, ((1,), (1,))) * SCALE
                top = jnp.maximum(top, jnp.max(past, axis=0, keepdims=True))
                past = jnp.exp(past - top)
            diag = jnp.exp(diag - top)
            total = jnp.sum(diag, axis=0, keepdims=True)
            if p:
                total = total + jnp.sum(past, axis=0, keepdims=True)
            share = 1.0 / total
            at = slice(head * HEAD_DIM, (head + 1) * HEAD_DIM)
            out = mm(vt_ref[at, done : done + rows], (diag * share).astype(BF))
            if p:
                out = out + mm(vt_ref[at, :done], (past * share).astype(BF))
            ot_ref[at] = out
            lse_ref[head : head + 1] = top + jnp.log(total)
        send_ref[...] = ot_ref[...].T.astype(BF)

    for p in range(ring):
        pl.when(block == p)(functools.partial(one, p))


def attend(qkv, where, heads):
    ring, pair, rows, full = qkv.shape
    width = full // 3
    return pl.pallas_call(
        functools.partial(attend_kernel, heads, ring),
        out_shape=(
            jax.ShapeDtypeStruct((ring * pair, rows, width), BF),
            jax.ShapeDtypeStruct((pair, ring, heads, rows), F32),
        ),
        grid_spec=pltpu.PrefetchScalarGridSpec(
            num_scalar_prefetch=1,
            grid=(pair, ring),
            in_specs=[pl.BlockSpec((ring, None, rows, full), lambda i, p, w: (0, i, 0, 0))],
            out_specs=[
                pl.BlockSpec((None, rows, width), lambda i, p, w: (p * pair + lax.rem(w[1] + i, pair), 0, 0)),
                pl.BlockSpec((None, None, heads, rows), lambda i, p, w: (i, p, 0, 0)),
            ],
            scratch_shapes=[
                pltpu.VMEM((ring * rows, width), BF),
                pltpu.VMEM((width, ring * rows), BF),
                pltpu.VMEM((width, rows), F32),
            ],
        ),
        compiler_params=pltpu.CompilerParams(vmem_limit_bytes=48 << 20),
        cost_estimate=pl.CostEstimate(flops=20 * 10**9, bytes_accessed=2 * qkv.size * 2, transcendentals=0),
        name="attend",
    )(where, qkv)


def attend_back_kernel(
    heads, ring, where_ref, qkv_ref, datt_ref, lse_ref, cos_ref, sin_ref, out_ref,
    key_ref, kt_ref, val_ref, qt_ref, dk_ref, dv_ref,
):
    rows, width = qkv_ref.shape[1], qkv_ref.shape[2] // 3
    half = width // 2
    block = pl.program_id(1)
    z = where_ref[0]

    @pl.when(block == 0)
    def _():
        for p in range(ring):
            at = lax.rem(z - p + ring, ring)
            key = qkv_ref[at, :, width : 2 * width]
            key_ref[p * rows : (p + 1) * rows] = key
            kt_ref[:, p * rows : (p + 1) * rows] = key.T
            val_ref[p * rows : (p + 1) * rows] = qkv_ref[at, :, 2 * width :]
        dk_ref[...] = jnp.zeros_like(dk_ref)
        dv_ref[...] = jnp.zeros_like(dv_ref)

    def turn_back(grad, p):
        cosine, sine = cos_ref[p * rows : (p + 1) * rows], sin_ref[p * rows : (p + 1) * rows]
        grad = grad.astype(BF).astype(F32)
        first, second = grad[:, :half], grad[:, half:]
        return (first * cosine + second * sine).astype(BF), (second * cosine - first * sine).astype(BF)

    def one(p):
        done = p * rows
        at = lax.rem(z - p + ring, ring)
        query = qkv_ref[at, :, :width]
        grad = datt_ref[...]
        keep = causal(rows)
        for head in range(heads):
            query_h = jnp.where(qk_head(width, head), query, jnp.zeros_like(query))
            grad_h = jnp.where(v_head(width, head), grad, jnp.zeros_like(grad))
            lse = lse_ref[head : head + 1]
            parts = []
            for low, high in ([(0, done)] if p else []) + [(done, done + rows)]:
                score = dot(key_ref[low:high], query_h, ((1,), (1,))) * SCALE
                prob = jnp.exp(score - lse)
                if low == done:
                    prob = jnp.where(keep, prob, 0.0)
                dprob = dot(val_ref[low:high], grad_h, ((1,), (1,)))
                parts.append((low, high, prob, dprob))
            delta = sum(jnp.sum(prob * dprob, axis=0, keepdims=True) for _, _, prob, dprob in parts)
            turned = 0.0
            for low, high, prob, dprob in parts:
                dscore = (prob * (dprob - delta)).astype(BF)
                key_t = jnp.concatenate(
                    [
                        kt_ref[head * HALF : (head + 1) * HALF, low:high],
                        kt_ref[half + head * HALF : half + (head + 1) * HALF, low:high],
                    ],
                    axis=0,
                )
                turned = turned + mm(key_t, dscore)
                dk_ref[low:high] += mm(dscore, query_h)
                dv_ref[low:high] += mm(prob.astype(BF), grad_h)
            qt_ref[head * HALF : (head + 1) * HALF] = turned[:HALF]
            qt_ref[half + head * HALF : half + (head + 1) * HALF] = turned[HALF:]
        first, second = turn_back(qt_ref[...].T * SCALE, p)
        out_ref[at, :, :half] = first
        out_ref[at, :, half:width] = second

    for p in range(ring):
        pl.when(block == p)(functools.partial(one, p))

    @pl.when(block == ring - 1)
    def _():
        for p in range(ring):
            at = lax.rem(z - p + ring, ring)
            first, second = turn_back(dk_ref[p * rows : (p + 1) * rows] * SCALE, p)
            out_ref[at, :, width : width + half] = first
            out_ref[at, :, width + half : 2 * width] = second
            out_ref[at, :, 2 * width :] = dv_ref[p * rows : (p + 1) * rows].astype(BF)


def attend_back(qkv, datt, lse, cosine, sine, where, heads):
    ring, pair, rows, full = qkv.shape
    width = full // 3
    return pl.pallas_call(
        functools.partial(attend_back_kernel, heads, ring),
        out_shape=jax.ShapeDtypeStruct(qkv.shape, BF),
        grid_spec=pltpu.PrefetchScalarGridSpec(
            num_scalar_prefetch=1,
            grid=(pair, ring),
            in_specs=[
                pl.BlockSpec((ring, None, rows, full), lambda i, p, w: (0, i, 0, 0)),
                pl.BlockSpec((None, rows, width), lambda i, p, w: (p * pair + lax.rem(w[1] + i, pair), 0, 0)),
                pl.BlockSpec((None, None, heads, rows), lambda i, p, w: (i, p, 0, 0)),
                pl.BlockSpec((ring * rows, width // 2), lambda i, p, w: (0, 0)),
                pl.BlockSpec((ring * rows, width // 2), lambda i, p, w: (0, 0)),
            ],
            out_specs=pl.BlockSpec((ring, None, rows, full), lambda i, p, w: (0, i, 0, 0)),
            scratch_shapes=[
                pltpu.VMEM((ring * rows, width), BF),
                pltpu.VMEM((width, ring * rows), BF),
                pltpu.VMEM((ring * rows, width), BF),
                pltpu.VMEM((width, rows), F32),
                pltpu.VMEM((ring * rows, width), F32),
                pltpu.VMEM((ring * rows, width), F32),
            ],
        ),
        compiler_params=pltpu.CompilerParams(vmem_limit_bytes=52 << 20),
        cost_estimate=pl.CostEstimate(flops=28 * 10**9, bytes_accessed=4 * qkv.size * 2, transcendentals=0),
        name="attend_back",
    )(where, qkv, datt, lse, cosine, sine)


def feed_kernel(
    steps, two_ref, two_other_ref, dout_ref, dout_other_ref, ff_in_ref, down_in_ref, ff_back_ref, down_out_ref, *refs,
):
    x_ref, dy_ref, hidden_ref, dff_ref, out_ref, out_other_ref, back_ref, back_other_ref = refs[-8:]
    rows = two_ref.shape[0]
    chunk = down_in_ref.shape[0]
    step = pl.program_id(0)

    @pl.when(step == 0)
    def _():
        x_ref[:rows], x_ref[rows:] = two_ref[...], two_other_ref[...]
        dy_ref[:rows], dy_ref[rows:] = dout_ref[...], dout_other_ref[...]

    def hidden_units(j):
        both = mm(x_ref[...], ff_in_ref[...])
        dhid = mm_nt(dy_ref[...], down_in_ref[...])
        gate, up = both[:, :chunk], both[:, chunk:]
        sig = jax.nn.sigmoid(gate)
        act = gate * sig
        hidden_ref[:, j * chunk : (j + 1) * chunk] = (act * up).astype(BF)
        dgate = dhid * up * (sig * (1.0 + gate * (1.0 - sig)))
        dff_ref[:, 2 * j * chunk : (2 * j + 1) * chunk] = dgate.astype(BF)
        dff_ref[:, (2 * j + 1) * chunk : (2 * j + 2) * chunk] = (dhid * act).astype(BF)

    for j in range(steps):
        pl.when(step == j)(functools.partial(hidden_units, j))

    @pl.when(step >= steps)
    def _():
        out = mm(hidden_ref[...], down_out_ref[...]).astype(BF)
        out_ref[...], out_other_ref[...] = out[:rows], out[rows:]
        back = mm_nt(dff_ref[...], ff_back_ref[...]).astype(BF)
        back_ref[...], back_other_ref[...] = back[:rows], back[rows:]


def feed(k, blocks, kept, two, two_other, dout, dout_other, ff_w, down_w, chunk):
    rows, model = two.shape
    ff = down_w.shape[0]
    steps = ff // chunk
    part = model // steps
    whole = pl.BlockSpec((rows, model), lambda j: (0, 0))
    share = pl.BlockSpec((rows, part), lambda j: (0, jnp.maximum(j - steps, 0)))
    widths = (model, model, ff, 2 * ff)
    *kept, out, out_other, back, back_other = pl.pallas_call(
        functools.partial(feed_kernel, steps),
        out_shape=[jax.ShapeDtypeStruct((blocks * 2 * rows, w), BF) for w in widths] + [jax.ShapeDtypeStruct((rows, model), BF)] * 4,
        grid=(2 * steps,),
        in_specs=[
            whole, whole, whole, whole,
            pl.BlockSpec((model, 2 * chunk), lambda j: (0, jnp.minimum(j, steps - 1))),
            pl.BlockSpec((chunk, model), lambda j: (jnp.minimum(j, steps - 1), 0)),
            pl.BlockSpec((part, 2 * ff), lambda j: (jnp.maximum(j - steps, 0), 0)),
            pl.BlockSpec((ff, part), lambda j: (0, jnp.maximum(j - steps, 0))),
        ] + [pl.BlockSpec(memory_space=pl.ANY)] * len(kept),
        out_specs=[pl.BlockSpec((2 * rows, w), lambda j: (k, 0)) for w in widths] + [share] * 4,
        input_output_aliases={8 + i: i for i in range(len(kept))},
        compiler_params=pltpu.CompilerParams(vmem_limit_bytes=56 << 20),
        cost_estimate=pl.CostEstimate(flops=2 * rows * model * ff * 6 // 4, bytes_accessed=1, transcendentals=0),
        name="feed",
    )(two, two_other, dout, dout_other, ff_w, down_w, ff_w, down_w, *kept)
    return kept, (out, out_other), (back, back_other)


def project_kernel(where_ref, one_ref, other_ref, w_ref, cos_ref, sin_ref, *refs):
    x_ref, out_ref = refs[-2:]
    rows = one_ref.shape[0]
    half = w_ref.shape[1] // 2
    step = pl.program_id(0)

    @pl.when(step == 0)
    def _():
        x_ref[:rows], x_ref[rows:] = one_ref[...], other_ref[...]

    flat = mm(x_ref[...], w_ref[...])

    @pl.when(step < 2)
    def _():
        cosine, sine = cos_ref[...], sin_ref[...]
        for i in range(2):
            first, second = flat[i * rows : (i + 1) * rows, :half], flat[i * rows : (i + 1) * rows, half:]
            out_ref[i, :, :half] = (first * cosine - second * sine).astype(BF)
            out_ref[i, :, half:] = (second * cosine + first * sine).astype(BF)

    @pl.when(step == 2)
    def _():
        out_ref[0], out_ref[1] = flat[:rows].astype(BF), flat[rows:].astype(BF)


def project(k, blocks, kept, where, one, other, w, cosine, sine):
    rows, model = cosine.shape[0] // blocks, one.shape[1]
    width = w.shape[1] // 3
    whole = pl.BlockSpec((rows, model), lambda j, at: (0, 0))
    table = pl.BlockSpec((rows, width // 2), lambda j, at: (lax.rem(at[0] - k + blocks, blocks), 0))
    return pl.pallas_call(
        project_kernel,
        out_shape=(
            jax.ShapeDtypeStruct((blocks * 2 * rows, model), BF),
            jax.ShapeDtypeStruct((blocks, 2, rows, 3 * width), BF),
        ),
        grid_spec=pltpu.PrefetchScalarGridSpec(
            num_scalar_prefetch=1,
            grid=(3,),
            in_specs=[whole, whole, pl.BlockSpec((model, width), lambda j, at: (0, j)), table, table]
            + [pl.BlockSpec(memory_space=pl.ANY)] * len(kept),
            out_specs=(
                pl.BlockSpec((2 * rows, model), lambda j, at: (k, 0)),
                pl.BlockSpec((None, 2, rows, width), lambda j, at: (k, 0, 0, j)),
            ),
        ),
        input_output_aliases={6 + i: i for i in range(len(kept))},
        compiler_params=pltpu.CompilerParams(vmem_limit_bytes=40 << 20),
        cost_estimate=pl.CostEstimate(flops=4 * rows * model * 3 * width, bytes_accessed=12 * rows * model, transcendentals=0),
        name="project",
    )(where, one, other, w, cosine, sine, *kept)


def ff_out_kernel(turn, gain_ref, gate_ref, up_ref, out_ref):
    pair = out_ref.shape[0]
    gain = gain_ref[...]
    for y in range(out_ref.shape[2] // (2 * turn)):
        for c in range(pair):
            at = (y * pair + c) * turn
            for i, ref in enumerate((gate_ref, up_ref)):
                cols = (ref[:, at : at + turn].astype(F32) * gain).astype(BF)
                out_ref[c, :, (2 * y + i) * turn : (2 * y + i + 1) * turn] = cols


def ff_out(ring, pair, turn, gain, w_gate, w_up):
    own, full = w_gate.shape
    part = pl.BlockSpec((own, full // ring), lambda s: (0, s))
    return pl.pallas_call(
        functools.partial(ff_out_kernel, turn),
        out_shape=jax.ShapeDtypeStruct((ring * pair, own, 2 * full // (ring * pair)), BF),
        grid=(ring,),
        in_specs=[pl.BlockSpec((own, 1), lambda s: (0, 0)), part, part],
        out_specs=pl.BlockSpec((pair, own, 2 * full // (ring * pair)), lambda s: (s, 0, 0)),
        cost_estimate=pl.CostEstimate(flops=1, bytes_accessed=8 * w_gate.size, transcendentals=0),
        name="ff_out",
    )(gain, w_gate, w_up)


def ff_back_kernel(turn, gain_ref, hat_ref, gate_ref, up_ref, gate_out, up_out, sum_ref):
    pair = hat_ref.shape[0]
    gain = gain_ref[...]
    total = jnp.zeros(gain.shape, F32)
    for y in range(hat_ref.shape[2] // (2 * turn)):
        for c in range(pair):
            at = (y * pair + c) * turn
            for i, (ref, out) in enumerate(((gate_ref, gate_out), (up_ref, up_out))):
                hat = hat_ref[c, :, (2 * y + i) * turn : (2 * y + i + 1) * turn].astype(F32)
                total += jnp.sum(hat * ref[:, at : at + turn].astype(F32), axis=1, keepdims=True)
                out[:, at : at + turn] = hat * gain

    @pl.when(pl.program_id(0) == 0)
    def _():
        sum_ref[...] = total

    @pl.when(pl.program_id(0) > 0)
    def _():
        sum_ref[...] += total


def ff_back(ring, turn, gain, hat, w_gate, w_up):
    own, full = w_gate.shape
    pair = hat.shape[0] // ring
    part = pl.BlockSpec((own, full // ring), lambda s: (0, s))
    column = pl.BlockSpec((own, 1), lambda s: (0, 0))
    return pl.pallas_call(
        functools.partial(ff_back_kernel, turn),
        out_shape=(jax.ShapeDtypeStruct((own, full), F32),) * 2 + (jax.ShapeDtypeStruct((own, 1), F32),),
        grid=(ring,),
        in_specs=[column, pl.BlockSpec((pair, *hat.shape[1:]), lambda s: (s, 0, 0)), part, part],
        out_specs=(part, part, column),
        cost_estimate=pl.CostEstimate(flops=1, bytes_accessed=16 * w_gate.size, transcendentals=0),
        name="ff_back",
    )(gain, hat, w_gate, w_up)


def qkv_out_kernel(gain_ref, query_ref, key_ref, value_ref, out_ref):
    width = query_ref.shape[1]
    gain = gain_ref[...]
    for i, ref in enumerate((query_ref, key_ref)):
        cols = ref[...].astype(F32) * gain
        parts = [cols[:, j : j + HALF] for start in (0, HALF) for j in range(start, width, HEAD_DIM)]
        out_ref[:, i * width : (i + 1) * width] = jnp.concatenate(parts, axis=1).astype(BF)
    out_ref[:, 2 * width :] = (value_ref[...].astype(F32) * gain).astype(BF)


def qkv_out(parts, gain, *ws):
    own, full = ws[0].shape
    width = full // parts
    return pl.pallas_call(
        qkv_out_kernel,
        out_shape=jax.ShapeDtypeStruct((parts, own, 3 * width), BF),
        grid=(parts,),
        in_specs=[pl.BlockSpec((own, 1), lambda t: (0, 0))] + [pl.BlockSpec((own, width), lambda t: (0, t))] * 3,
        out_specs=pl.BlockSpec((None, own, 3 * width), lambda t: (t, 0, 0)),
        cost_estimate=pl.CostEstimate(flops=1, bytes_accessed=12 * ws[0].size, transcendentals=0),
        name="qkv_out",
    )(gain, *ws)


def qkv_back_kernel(gain_ref, hat_ref, query_ref, key_ref, value_ref, query_out, key_out, value_out, sum_ref):
    width = query_ref.shape[1]
    gain = gain_ref[...]
    total = jnp.zeros(gain.shape, F32)
    for i, (ref, out) in enumerate(((query_ref, query_out), (key_ref, key_out), (value_ref, value_out))):
        hat = hat_ref[:, i * width : (i + 1) * width].astype(F32)
        if i < 2:
            parts = [hat[:, j : j + HALF] for at in range(0, width // 2, HALF) for j in (at, width // 2 + at)]
            hat = jnp.concatenate(parts, axis=1)
        total += jnp.sum(hat * ref[...].astype(F32), axis=1, keepdims=True)
        out[...] = hat * gain

    @pl.when(pl.program_id(0) == 0)
    def _():
        sum_ref[...] = total

    @pl.when(pl.program_id(0) > 0)
    def _():
        sum_ref[...] += total


def qkv_back(gain, hat, *ws):
    own, full = ws[0].shape
    parts = hat.shape[0]
    width = full // parts
    part = pl.BlockSpec((own, width), lambda t: (0, t))
    column = pl.BlockSpec((own, 1), lambda t: (0, 0))
    return pl.pallas_call(
        qkv_back_kernel,
        out_shape=(jax.ShapeDtypeStruct((own, full), F32),) * 3 + (jax.ShapeDtypeStruct((own, 1), F32),),
        grid=(parts,),
        in_specs=[column, pl.BlockSpec((None, own, 3 * width), lambda t: (t, 0, 0)), part, part, part],
        out_specs=(part, part, part, column),
        cost_estimate=pl.CostEstimate(flops=1, bytes_accessed=24 * ws[0].size, transcendentals=0),
        name="qkv_back",
    )(gain, hat, *ws)


def after(value, *others):
    return lax.optimization_barrier((value, *others))[0] if others else value


def unit(values):
    inverse = lax.rsqrt(jnp.mean(values * values, axis=1, keepdims=True) + EPS)
    return values * inverse, inverse


def unit_back(grad, normed, inverse):
    return inverse * (grad - normed * jnp.mean(grad * normed, axis=1, keepdims=True))


def local(ring, plane, pair, inputs, norm1_gain, w_query, w_key, w_value, w_output, norm2_gain, w_gate, w_up, w_down, out_grad):
    seq_count, rows, model = inputs.shape
    parts = ring * pair
    own = w_query.shape[0]
    ff_own = w_down.shape[0]
    width = model // parts
    heads = width // HEAD_DIM
    half = width // 2
    ff = plane * ff_own
    group = ("seq", "core")
    z = lax.axis_index("seq")
    c = lax.axis_index("core")
    where = jnp.stack([z, c]).astype(jnp.int32)
    ring_pairs = [(i, (i + 1) % ring) for i in range(ring)]
    core_pairs = [(i, (i + 1) % pair) for i in range(pair)]

    def hop(x):
        return lax.ppermute(x, "seq", ring_pairs)

    def swap(x):
        return lax.ppermute(x, "core", core_pairs)

    def ring_sum(shares, *fill):
        total = shares[1].astype(BF)
        for k in range(2, ring):
            total = (hop(total).astype(F32) + shares[k]).astype(BF)
            total = after(total, *fill[k - 2 : k - 1])
        return hop(total).astype(F32) + shares[0]

    def both_cores(term):
        return term[0].astype(F32) + swap(term[1]).astype(F32)

    def exchange(x):
        return lax.all_to_all(x, group, 0, 0, tiled=True)

    def exchange_rows(x):
        return exchange(x).reshape(ring, pair * own, x.shape[2])

    def gather_rows(x):
        return lax.all_gather(x, "yx", axis=1, tiled=True).reshape(model, x.shape[2])

    def sum_rows(x):
        x = x.reshape(ring, plane * pair * own, x.shape[1])
        return lax.psum_scatter(x, "yx", scatter_dimension=1, tiled=True)

    def return_rows(x):
        return exchange(x.reshape(parts, own, x.shape[2]))

    gain_one, gain_two = norm1_gain.astype(F32)[:, None], norm2_gain.astype(F32)[:, None]

    residual = inputs.reshape(rows, model).astype(F32)
    normed_one, inverse_one = unit(residual)
    one = jnp.concatenate([normed_one.astype(BF), w_output])
    qkv_w = qkv_out(parts, gain_one, w_query, w_key, w_value)
    ff_w = ff_out(ring, pair, ff_own, gain_two, w_gate, w_up)
    down_w = lax.all_gather(w_down, "yx", axis=0, tiled=True)
    ones = [one, hop(one)]
    qkv_w = exchange_rows(after(qkv_w, ones[1]))
    qkv_sent, qkv_w = qkv_w, gather_rows(after(qkv_w, down_w))
    for k in range(1, ring - 1):
        ones.append(hop(after(ones[k], qkv_sent if k == 1 else ff_w, *([qkv_w] if k == ring - 2 else []))))
    ff_w = exchange_rows(after(ff_w, ones[-1], qkv_w))
    output_w = jnp.stack([ones[k][rows:] for k in reversed(range(ring))] * 2)
    output_w = lax.dynamic_slice_in_dim(output_w, ring - 1 - z, ring)
    output_w = lax.all_gather(output_w, ("yx", "core"), axis=1, tiled=True).reshape(model, model)

    freqs = jnp.exp(jnp.arange(HALF, dtype=F32) * (-2.0 * math.log(ROPE_BASE) / HEAD_DIM))
    angle = jnp.arange(ring * rows, dtype=jnp.int32).astype(F32)[:, None] * freqs[None, :]
    cosine, sine = jnp.tile(jnp.cos(angle), (1, heads)), jnp.tile(jnp.sin(angle), (1, heads))
    kept = []
    for k in range(ring):
        kept = project(k, ring, kept, where, ones[k], swap(ones[k]), qkv_w, cosine, sine)
    all_ones, qkv = kept
    att_send, lse = attend(qkv, where, heads)
    att_send, ff_w = lax.optimization_barrier((att_send, ff_w))
    ff_w = gather_rows(ff_w)
    att = exchange(att_send).transpose(1, 0, 2).reshape(rows, model)
    mid = residual + mm(att, output_w)

    normed_two, inverse_two = unit(mid)
    twos = [normed_two.astype(BF)]
    grad_out = out_grad.reshape(rows, model)
    douts = [grad_out, hop(after(grad_out, att))]
    for k in range(1, ring):
        twos.append(hop(twos[-1]))
        if k < ring - 1:
            douts.append(hop(after(douts[-1], att if k == 1 else twos[k - 1])))
    kept, out_terms = [], [None] * ring
    for k in [1, 0, *range(2, ring)]:
        if k == 2:
            total = first_share
        two = after(twos[k], total) if k > 1 else twos[k]
        kept, out_terms[k], back = feed(k, ring, kept, two, swap(twos[k]), douts[k], swap(douts[k]), ff_w, down_w, ff_own)
        if k == 0:
            own_share = both_cores(back)
        elif k == 1:
            first_share = both_cores(back).astype(BF)
        else:
            here = hop(total).astype(F32) + back[0].astype(F32)
            here = after(here, own_share)
            total = (here + swap(back[1]).astype(F32)).astype(BF)
    tokens = ring * pair * rows
    all_twos, all_douts, hiddens, dffs = kept
    ff_grad = mm_tn(after(all_twos, total), dffs).astype(BF)
    grad_two = after(hop(total).astype(F32) + own_share, ff_grad)
    ff_grad = sum_rows(after(ff_grad, grad_two))

    grad_mid = grad_out.astype(F32) + unit_back(grad_two, normed_two, inverse_two)
    proj = grad_mid.astype(BF)
    datt = mm_nt(proj, output_w).astype(BF)
    datt = datt.reshape(rows, parts, width).transpose(1, 0, 2)

    split = model // pair
    mine = lax.dynamic_slice_in_dim(att, c * split, split, axis=1)
    others = swap(lax.dynamic_slice_in_dim(att, (pair - 1 - c) * split, split, axis=1))
    output_grad = mm_tn(jnp.concatenate([mine, others]), jnp.concatenate([proj, swap(proj)])).astype(BF)
    shares = [both_cores(after(t, grad_two)) for t in out_terms]
    total = (hop(shares[1].astype(BF)).astype(F32) + shares[2]).astype(BF)
    datt = after(exchange(datt), output_grad, total)
    dqkv = attend_back(qkv, datt, lse, cosine, sine, where, heads)
    total = after(total, datt)
    for k in range(3, ring):
        total = (hop(total).astype(F32) + shares[k]).astype(BF)
    dqkv = after(dqkv, ff_grad, total)
    output = (mid + (hop(total).astype(F32) + shares[0])).astype(BF).reshape(inputs.shape)
    ff_grad = return_rows(ff_grad)
    gate_grad, up_grad, gain_two_grad = ff_back(ring, ff_own, gain_two, ff_grad, w_gate, w_up)

    qkv_grad = mm_tn(all_ones, dqkv.reshape(tokens, 3 * width)).astype(BF)
    dqkv = after(dqkv, qkv_grad)
    down_grad = mm_tn(hiddens, after(all_douts, dqkv)).astype(BF)
    down_grad = lax.psum_scatter(down_grad, "yx", scatter_dimension=0, tiled=True).astype(F32)
    qkv_grad = sum_rows(qkv_grad)
    one_terms = [[mm_nt(dqkv[k, i], qkv_w).astype(BF) for i in range(pair)] for k in range(ring)]
    shares = [both_cores(t) for t in one_terms]
    total = (hop(shares[1].astype(BF)).astype(F32) + shares[2]).astype(BF)
    output_grad = lax.psum_scatter(after(output_grad, one_terms[1][0]), "yx", scatter_dimension=0, tiled=True)
    qkv_grad = return_rows(qkv_grad)
    total, qkv_grad, gate_grad, up_grad, gain_two_grad, output = lax.optimization_barrier(
        (total, qkv_grad, gate_grad, up_grad, gain_two_grad, output)
    )
    query_grad, key_grad, value_grad, gain_one_grad = qkv_back(gain_one, qkv_grad, w_query, w_key, w_value)
    for k in range(3, ring):
        total = (hop(total).astype(F32) + shares[k]).astype(BF)
    output_grad = after(output_grad, total).reshape(ring, own, model)
    output_grad = ring_sum(
        [lax.dynamic_index_in_dim(output_grad, lax.rem(z - k + ring, ring), keepdims=False).astype(F32) for k in range(ring)]
    ).astype(BF)
    moves = [((s * plane + y) * pair + h, (h * plane + y) * ring + s) for s in range(ring) for y in range(plane) for h in range(pair)]
    output_grad = lax.ppermute(output_grad, ("seq", "yx", "core"), moves).astype(F32)
    grad_one = hop(total).astype(F32) + shares[0]
    input_grad = (grad_mid + unit_back(grad_one, normed_one, inverse_one)).reshape(inputs.shape)
    return (
        output,
        input_grad,
        gain_one_grad[:, 0],
        query_grad,
        key_grad,
        value_grad,
        output_grad,
        gain_two_grad[:, 0],
        gate_grad,
        up_grad,
        down_grad,
    )


def solution(mesh):
    ring, fsdp = mesh.shape["seq"], mesh.shape["fsdp"]
    pair = 2
    plane = fsdp // pair
    fine = Mesh(mesh.devices.reshape(ring, plane, pair), ("seq", "yx", "core"))
    tokens = P(("yx", "core"), "seq", None)
    every = ("seq", "yx", "core")
    weight, gain = P(every, None), P(every)
    return jax.shard_map(
        functools.partial(local, ring, plane, pair),
        mesh=fine,
        in_specs=(tokens, gain, weight, weight, weight, weight, gain, weight, weight, weight, tokens),
        out_specs=(tokens, tokens, gain, weight, weight, weight, weight, gain, weight, weight, weight),
        check_vma=False,
    )
```
